32 devices in a mesh: comp: 8 (over z, y), harm: 4 (over x, core).
Axes of the slice: x: 2, y: 2, z: 4, core: 2. Of those that a mesh axis runs over, the one named last changes fastest.
Arguments:
- load: float32 [128, 32768], P('harm', 'comp'), may hold values from -6 to 6
- stiff_blocks: bfloat16 [256, 8, 128, 128], P('comp'), as said below
- mass_blocks: bfloat16 [256, 8, 128, 128], P('comp'), as said below
- block_cols: int32 [256, 8], P('comp'), may hold values from -8 to 263, as said below
- contact_rows: int32 [8, 256], P('comp'), may hold values from 0 to 4095, as said below
- partner_slot: int32 [8, 256], P('comp'), may hold values from 0 to 255, each once within a row
- contact_count: int32 [8], P('comp'), may hold values from 32 to 256, as said below
- normal_load: float32 [8, 256], P('comp'), may hold values from 0.3 to 3
- contact_stiffness: float32 [8, 256], P('comp'), may hold values from 0.3 to 3
- frequency: float32 [1], replicated, may hold values from 0.2 to 1
Outputs:
- displacement: float32 [128, 32768], P('harm', 'comp')
- residual: float32 [128, 32768], P('harm', 'comp')
The draws below stay inside these ranges and needn't reach their ends.
Inputs may be any that keep to these rules, and one draw needn't show every extreme that they name: `block_cols`: entry 0 of block row r is r; its other 7 entries are distinct, differ from r by 1 to 8, and include r - 8 and r + 8; columns outside 0 .. 255 refer to zero parts of the field. `contact_rows`: the 256 entries of one group are distinct. Slots 0 .. contact_count[d]-1 of group d are live; the others carry no force. `stiff_blocks`: slot 0 of every block row is the block on the diagonal. `mass_blocks`: slot 0 of every block row is the block on the diagonal.
All inputs are finite; a program needn't handle non-finite values.
Results may differ from the reference program's by a relative error of at most 0.015.
The reference program's roundings to bfloat16 on the way (of `rounded`) count: a program that leaves them out, or rounds other values in their place, can miss the bound.
Values may be sent and summed in bfloat16 or wider, within the bound.
A program may use at most 64 MiB of HBM per device.

```python
import math
import jax
import jax.numpy as jnp
from jax import lax

H = 128
TIME_POINTS = 1024
BLK = 128
SLOTS = 8
BAND = 8
ITERS = 3
CMAX = 256
GROUPS = 8
NB = 256
DOF_DEV = 4096
NDOF = 32768


def block_draw(key, lowest, highest, spread):
    key_one, key_two = jax.random.split(key)
    values = jnp.clip(jax.random.normal(key_one, (NB, SLOTS, BLK, BLK), jnp.float32), -6.0, 6.0)
    values = values * (spread / math.sqrt(SLOTS * BLK))
    diagonal = jax.random.uniform(key_two, (NB, BLK), jnp.float32, lowest, highest)
    values = values.at[:, 0].add(diagonal[:, :, None] * jnp.eye(BLK, dtype=jnp.float32)[None, :, :])
    return values.astype(jnp.bfloat16)


def draw_stiff_blocks(key, part):
    return block_draw(jax.random.fold_in(key, 11), 3.0, 5.0, 1.0)


def draw_mass_blocks(key, part):
    return block_draw(jax.random.fold_in(key, 23), 0.5, 1.0, 0.25)


def draw_block_cols(key, part):
    row_ids = jnp.arange(NB, dtype=jnp.int32)
    offset_pool = jnp.concatenate([jnp.arange(1 - BAND, 0, dtype=jnp.int32), jnp.arange(1, BAND, dtype=jnp.int32)])

    def one_row(row_key):
        pick_key, order_key = jax.random.split(row_key)
        picked = jax.random.permutation(pick_key, offset_pool)[:SLOTS - 3]
        others = jnp.concatenate([jnp.array([-BAND, BAND], jnp.int32), picked])
        return jnp.concatenate([jnp.zeros((1,), jnp.int32), jax.random.permutation(order_key, others)])
    offsets = jax.vmap(one_row)(jax.random.split(jax.random.fold_in(key, 31), NB))
    return row_ids[:, None] + offsets


def draw_contact_rows(key, part):
    key_one, key_two = jax.random.split(jax.random.fold_in(key, 41))
    inner_rows = jnp.arange(1, DOF_DEV - 1, dtype=jnp.int32)

    def one_device(device_key):
        pick_key, order_key, drawn_key = jax.random.split(device_key, 3)
        drawn_rows = jax.random.permutation(drawn_key, jnp.arange(DOF_DEV, dtype=jnp.int32))[:CMAX]
        chosen = jax.random.permutation(pick_key, inner_rows)[:CMAX - 2]
        with_ends = jnp.concatenate([jnp.array([0, DOF_DEV - 1], jnp.int32), chosen])
        return (drawn_rows, jax.random.permutation(order_key, with_ends))
    drawn_rows, ended = jax.vmap(one_device)(jax.random.split(key_one, GROUPS))
    marked = jax.random.randint(key_two, (), 0, GROUPS)
    return jnp.where((jnp.arange(GROUPS, dtype=jnp.int32) == marked)[:, None], ended, drawn_rows)


def draw_contact_count(key, part):
    key_one, key_two, key_three, key_four = jax.random.split(jax.random.fold_in(key, 53), 4)
    counts = jax.random.randint(key_one, (GROUPS,), CMAX // 8, CMAX // 2 + 1)
    heavy = jax.random.randint(key_two, (GROUPS,), 0, 8) == 0
    counts = jnp.where(heavy, CMAX, counts)
    busiest = jax.random.randint(key_three, (), 0, GROUPS)
    lightest = (busiest + 1 + jax.random.randint(key_four, (), 0, GROUPS - 1)) % GROUPS
    counts = counts.at[busiest].set(CMAX).at[lightest].set(CMAX // 8)
    return counts.astype(jnp.int32)


def block_levels(key, dims, pieces, low, largest):
    loudness, own = 1.0, jax.random.fold_in(key, 6)
    for axis_at, parts in pieces:
        draws = jnp.exp(jax.random.uniform(jax.random.fold_in(own, axis_at), (parts,), jnp.float32, low / len(pieces), largest / len(pieces)))
        loudness = loudness * jnp.repeat(draws, dims[axis_at] // parts).reshape([-1 if axis == axis_at else 1 for axis in range(len(dims))])
    return loudness


def centred(key, extent, width, most, cuts=(), held_as=jnp.bfloat16):
    entries = width * jax.random.normal(key, extent, jnp.float32)
    if cuts:
        entries = entries * block_levels(key, extent, cuts, -0.22, 0.18)
    return jnp.clip(entries, -most, most).astype(held_as)


def setup_inputs(seed: int = 0) -> dict:
    splits = jax.random.split(jax.random.key(seed), 11)
    load = centred(splits[0], (H, NDOF), 1.0, 6.0, ((0, 4), (1, 8)), jnp.float32)
    stiff_blocks = draw_stiff_blocks(jax.random.fold_in(splits[10], 71), 0)
    mass_blocks = draw_mass_blocks(jax.random.fold_in(splits[10], 71), 0)
    block_cols = draw_block_cols(jax.random.fold_in(splits[10], 71), 0)
    contact_rows = draw_contact_rows(jax.random.fold_in(splits[10], 71), 0)
    partner_slot = jax.vmap(lambda own: jax.random.permutation(own, CMAX))(jax.random.split(splits[5], GROUPS)).reshape((GROUPS, CMAX)).astype(jnp.int32)
    contact_count = draw_contact_count(jax.random.fold_in(splits[10], 71), 0)
    normal_load = jnp.clip(jnp.exp(math.log(3.0) - 2.3025851 * jax.random.uniform(splits[7], (GROUPS, CMAX), jnp.float32) ** block_levels(splits[7], (GROUPS, CMAX), ((0, 8),), -0.2, 0.2)), 0.3, 3.0)
    contact_stiffness = jnp.clip(jnp.exp(math.log(3.0) - 2.3025851 * jax.random.uniform(splits[8], (GROUPS, CMAX), jnp.float32) ** block_levels(splits[8], (GROUPS, CMAX), ((0, 8),), -0.2, 0.2)), 0.3, 3.0)
    frequency = jnp.clip(jax.random.uniform(splits[9], (1,), jnp.float32, 0.2, 1.0), 0.2, 1.0)
    return dict(load=load, stiff_blocks=stiff_blocks, mass_blocks=mass_blocks, block_cols=block_cols, contact_rows=contact_rows, partner_slot=partner_slot, contact_count=contact_count, normal_load=normal_load, contact_stiffness=contact_stiffness, frequency=frequency)


def harmonic_tables():
    column_list = jnp.arange(H, dtype=jnp.int32)
    harmonic_orders = jnp.where(column_list <= H // 2, column_list, column_list - H // 2).astype(jnp.int32)
    time_points = jnp.arange(TIME_POINTS, dtype=jnp.int32)
    phase_values = (time_points[:, None] * harmonic_orders[None, :]) % TIME_POINTS
    phase_angles = phase_values.astype(jnp.float32) * jnp.float32(2.0 * math.pi / TIME_POINTS)
    instant_table = jnp.where(column_list[None, :] <= H // 2, jnp.cos(phase_angles), jnp.sin(phase_angles))
    weight_factors = jnp.where(column_list == 0, jnp.float32(1.0), jnp.float32(2.0)).astype(jnp.float32) / jnp.float32(TIME_POINTS)
    return instant_table, weight_factors, harmonic_orders


def block_products(stiff_blocks, mass_blocks, block_cols, rounded):
    padded = jnp.pad(rounded.reshape(H, NB, BLK), ((0, 0), (BAND, BAND), (0, 0))).astype(jnp.float32)

    def one_row(row_index):
        stiff_row = stiff_blocks[row_index].astype(jnp.float32)
        mass_row = mass_blocks[row_index].astype(jnp.float32)
        column_row = (block_cols[row_index] + BAND).astype(jnp.int32)
        picked = jnp.take(padded, column_row, axis=1)
        stiff_out = jnp.einsum("sij,hsj->hi", stiff_row, picked, precision=lax.Precision.HIGHEST)
        mass_out = jnp.einsum("sij,hsj->hi", mass_row, picked, precision=lax.Precision.HIGHEST)
        return stiff_out, mass_out

    stiff_all, mass_all = lax.map(one_row, jnp.arange(NB, dtype=jnp.int32))
    stiff_part = jnp.transpose(stiff_all, (1, 0, 2)).reshape(H, NB * BLK)
    mass_part = jnp.transpose(mass_all, (1, 0, 2)).reshape(H, NB * BLK)
    return stiff_part, mass_part


def contact_force(displacement, contact_rows, partner_slot, contact_count, normal_load, contact_stiffness, instant_table, weight_factors):
    shaped = displacement.reshape(H, GROUPS, DOF_DEV)
    listed = jnp.take_along_axis(shaped, contact_rows[None, :, :].astype(jnp.int32), axis=2)
    partner_ids = jnp.bitwise_xor(jnp.arange(GROUPS, dtype=jnp.int32), jnp.int32(GROUPS // 2))
    facing = jnp.take_along_axis(jnp.take(listed, partner_ids, axis=1), partner_slot[None, :, :].astype(jnp.int32), axis=2)
    relative = (listed - facing).reshape(H, GROUPS * CMAX)
    time_values = jnp.dot(instant_table, relative, precision=lax.Precision.HIGHEST)
    load_part = normal_load.reshape(1, GROUPS * CMAX)
    stiff_part = contact_stiffness.reshape(1, GROUPS * CMAX)
    live_mask = (jnp.arange(CMAX, dtype=jnp.int32)[None, :] < contact_count[:, None]).reshape(1, GROUPS * CMAX)
    forces = jnp.where(live_mask, load_part * jnp.tanh(stiff_part * time_values / load_part), jnp.zeros_like(time_values))
    projected = lax.dot_general(instant_table, forces, (((0,), (0,)), ((), ())), precision=lax.Precision.HIGHEST) * weight_factors[:, None]
    targets = (jnp.arange(GROUPS, dtype=jnp.int32)[:, None] * DOF_DEV + contact_rows.astype(jnp.int32)).reshape(GROUPS * CMAX)
    return jnp.zeros((H, NDOF), projected.dtype).at[:, targets].add(projected)


def reference(load, stiff_blocks, mass_blocks, block_cols, contact_rows, partner_slot, contact_count, normal_load, contact_stiffness, frequency):
    instant_table, weight_factors, harmonic_orders = harmonic_tables()
    factor = frequency[0] * harmonic_orders.astype(jnp.float32) * jnp.float32(2.0 / H)
    factor = factor * factor
    stiff_diag = jnp.diagonal(stiff_blocks[:, 0], axis1=1, axis2=2).astype(jnp.float32).reshape(NDOF)
    mass_diag = jnp.diagonal(mass_blocks[:, 0], axis1=1, axis2=2).astype(jnp.float32).reshape(NDOF)
    dynamic = stiff_diag[None, :] - factor[:, None] * mass_diag[None, :]
    displacement = load / dynamic
    residual = jnp.zeros_like(displacement)
    for sweep_index in range(ITERS):
        rounded = displacement.astype(jnp.bfloat16)
        gap = displacement - lax.optimization_barrier(rounded).astype(jnp.float32)
        stiff_part, mass_part = block_products(stiff_blocks, mass_blocks, block_cols, rounded)
        stiff_part = stiff_part + stiff_diag[None, :] * gap
        mass_part = mass_part + mass_diag[None, :] * gap
        applied = stiff_part - factor[:, None] * mass_part
        nonlinear = contact_force(displacement, contact_rows, partner_slot, contact_count, normal_load, contact_stiffness, instant_table, weight_factors)
        residual = load - applied - nonlinear
        displacement = displacement + residual / dynamic
    return displacement, residual
```

```python
import functools
import math

import jax
import jax.numpy as jnp
import numpy as np
from jax import lax
from jax.experimental import pallas as pl
from jax.experimental.pallas import tpu as pltpu
from jax.sharding import PartitionSpec as P

H = 128
TIME_POINTS = 1024
BAND = 8
ITERS = 3
MESH = pl.DeviceIdType.MESH
F32 = jnp.float32
BF16 = jnp.bfloat16
NN = (((1,), (0,)), ((), ()))
NT = (((1,), (1,)), ((), ()))


def host_tables(harm_parts):
    column = np.arange(H)
    orders = np.where(column <= H // 2, column, column - H // 2)
    phase = np.arange(TIME_POINTS)[:, None] * orders[None, :] % TIME_POINTS
    angle = phase * (2.0 * math.pi / TIME_POINTS)
    table = np.where(column[None, :] <= H // 2, np.cos(angle), np.sin(angle))
    table = table.astype(np.float32)
    high = table.astype(BF16)
    low = (table - high.astype(np.float32)).astype(BF16)
    to_time = np.concatenate([high, high], axis=1)
    back = np.stack(
        [high.T.reshape(harm_parts, -1, TIME_POINTS), low.T.reshape(harm_parts, -1, TIME_POINTS)], axis=1
    )
    return to_time, back.reshape(harm_parts, -1, TIME_POINTS)


def halves(value):
    high = value.astype(BF16)
    low = (value - high.astype(F32)).astype(BF16)
    return high, low


def stacked(value):
    return jnp.concatenate(halves(value), axis=0)


def folded(value):
    half = value.shape[0] // 2
    return value[:half] + value[half:]


def product(left, right, dims):
    return lax.dot_general(left, right, dims, preferred_element_type=F32)


def kernel(
    comp_size,
    harm_size,
    load_hbm,
    stiff_hbm,
    mass_hbm,
    cols_hbm,
    rows_hbm,
    partner_hbm,
    count_ref,
    normal_hbm,
    spring_hbm,
    freq_ref,
    time_hbm,
    back_hbm,
    disp_out,
    res_out,
    cols_ref,
    rows_ref,
    partner_ref,
    normal_ref,
    spring_ref,
    factor_ref,
    load_ref,
    time_ref,
    back_ref,
    stiff_ref,
    mass_ref,
    field,
    shift,
    dyn_ref,
    inv_ref,
    slot_inverse,
    hot,
    perm,
    ext,
    halo,
    listed_ref,
    sent_ref,
    shared,
    relative_ref,
    rel_parts,
    small_sem,
    side_sem,
    diag_sem,
    block_sem,
    halo_send,
    halo_recv,
    share_send,
    share_recv,
):
    comp = lax.axis_index("comp")
    harm = lax.axis_index("harm")
    block_rows = stiff_ref.shape[0]
    slots = stiff_ref.shape[1]
    blk = stiff_ref.shape[2]
    nh = load_ref.shape[0]
    wide = 2 * blk
    pairs = block_rows // 2
    chunks = block_rows // BAND
    cmax = rows_ref.shape[1]
    first_row = comp * block_rows
    has_prev = comp > 0
    has_next = comp < comp_size - 1
    after = lax.rem(comp + 1, comp_size)
    before = lax.rem(comp + comp_size - 1, comp_size)
    facing = lax.rem(comp + comp_size // 2, comp_size)
    order = list(range(1, chunks - 1)) + [0, chunks - 1]

    small_copies = [
        pltpu.make_async_copy(source, held, small_sem.at[i])
        for i, (source, held) in enumerate(
            (
                (rows_hbm, rows_ref),
                (partner_hbm, partner_ref),
                (normal_hbm, normal_ref),
                (spring_hbm, spring_ref),
                (cols_hbm, cols_ref),
            )
        )
    ]
    for copy in small_copies:
        copy.start()
    diag_copies = [
        pltpu.make_async_copy(source.at[:, pl.ds(0, 1)], held.at[:, pl.ds(0, 1)], diag_sem.at[i])
        for i, (source, held) in enumerate(((stiff_hbm, stiff_ref), (mass_hbm, mass_ref)))
    ]
    for copy in diag_copies:
        copy.start()
    load_copy, *table_copies = [
        pltpu.make_async_copy(source, held, side_sem.at[i])
        for i, (source, held) in enumerate(
            ((load_hbm, load_ref), (time_hbm, time_ref), (back_hbm, back_ref))
        )
    ]
    load_copy.start()
    block_copies = {}
    for c in order:
        span = (pl.ds(c * BAND, BAND), pl.ds(1, slots - 1))
        block_copies[c] = [
            pltpu.make_async_copy(source.at[span], held.at[span], block_sem.at[c, i])
            for i, (source, held) in enumerate(((stiff_hbm, stiff_ref), (mass_hbm, mass_ref)))
        ]
        for copy in block_copies[c]:
            copy.start()
    for copy in table_copies:
        copy.start()

    barrier = pltpu.get_barrier_semaphore()
    partners = [(comp, lax.rem(harm + step, harm_size)) for step in range(1, harm_size)]
    partners += [(facing, lax.rem(harm + step, harm_size)) for step in range(harm_size)]
    for partner in partners:
        pl.semaphore_signal(barrier, inc=1, device_id=partner, device_id_type=MESH)

    @pl.when(has_prev)
    def _():
        pl.semaphore_signal(barrier, inc=1, device_id=(before, harm), device_id_type=MESH)

    @pl.when(has_next)
    def _():
        pl.semaphore_signal(barrier, inc=1, device_id=(after, harm), device_id_type=MESH)

    for copy in small_copies:
        copy.wait()

    row_list = rows_ref[...]
    sub = lax.broadcasted_iota(jnp.int32, (wide, cmax), 0)

    def mark(p, carry):
        base = pl.multiple_of(p * wide, wide)
        hot[pl.ds(base, wide), :] = jnp.where(sub == row_list - base, 1.0, 0.0).astype(BF16)
        return carry

    lax.fori_loop(0, pairs, mark, 0, unroll=2)
    slot_axis = lax.broadcasted_iota(jnp.int32, (cmax, cmax), 0)
    perm[...] = jnp.where(slot_axis == partner_ref[...], 1.0, 0.0).astype(BF16)
    ext[pl.ds(0, BAND)] = jnp.zeros((BAND, nh, blk), BF16)
    ext[pl.ds(BAND + block_rows, BAND)] = jnp.zeros((BAND, nh, blk), BF16)

    def factor_of(width):
        index = harm * nh + lax.broadcasted_iota(jnp.int32, (nh, width), 0)
        wave = jnp.where(index <= H // 2, index, index - H // 2).astype(F32)
        value = freq_ref[0] * wave * (2.0 / H)
        return value * value

    factor_ref[...] = factor_of(wide)
    slot_index = lax.broadcasted_iota(jnp.int32, (1, cmax), 1)
    slot_scale = jnp.where(slot_index < count_ref[0], normal_ref[...], 0.0)
    own_index = harm * nh + lax.broadcasted_iota(jnp.int32, (nh, cmax), 0)
    own_weight = jnp.where(own_index == 0, 1.0 / TIME_POINTS, 2.0 / TIME_POINTS)
    spring_ratio = spring_ref[...] / normal_ref[...]

    for copy in diag_copies:
        copy.wait()
    load_copy.wait()
    eye = lax.broadcasted_iota(jnp.int32, (blk, blk), 0) == lax.broadcasted_iota(
        jnp.int32, (blk, blk), 1
    )

    def diagonal(ref, p):
        parts = [
            jnp.sum(jnp.where(eye, ref[2 * p + q, 0].astype(F32), 0.0), axis=0, keepdims=True)
            for q in range(2)
        ]
        return jnp.concatenate(parts, axis=1)

    def put_rounded(p, value):
        rounded = value.astype(BF16)
        for q in range(2):
            ext[BAND + 2 * p + q] = rounded[:, q * blk : (q + 1) * blk]

    def lanes(p):
        return pl.ds(pl.multiple_of(p * wide, wide), wide)

    def start_field(p, gathered):
        stiff_diag = diagonal(stiff_ref, p)
        mass_diag = diagonal(mass_ref, p)
        dynamic = stiff_diag - factor_ref[...] * mass_diag
        inverse = 1.0 / dynamic
        value = load_ref[:, lanes(p)] * inverse
        dyn_ref[p] = dynamic
        inv_ref[p] = inverse
        field[p] = value
        put_rounded(p, value)
        high, low = halves(value)
        diagonals = jnp.concatenate(
            [jnp.broadcast_to(part, (8, wide)) for part in (stiff_diag, mass_diag)], axis=0
        )
        left = jnp.concatenate([high, low, diagonals.astype(BF16)], axis=0)
        return gathered + product(left, hot[lanes(p), :], NN)

    gathered = lax.fori_loop(
        0, pairs, start_field, jnp.zeros((2 * nh + 16, cmax), F32), unroll=4
    )
    listed = folded(gathered[: 2 * nh])
    slot_dynamic = gathered[2 * nh : 2 * nh + 1] - factor_of(cmax) * gathered[2 * nh + 8 : 2 * nh + 9]
    slot_inverse[...] = 1.0 / slot_dynamic

    neighbours = jnp.minimum(comp, 1) + jnp.minimum(comp_size - 1 - comp, 1)
    pl.semaphore_wait(barrier, len(partners) + neighbours)

    def apply_rows(first, stop, gathered):
        def body(p, carry):
            applied = []
            for q in range(2):
                r = 2 * p + q
                picked = jnp.concatenate(
                    [
                        ext[jnp.clip(cols_ref[s, r] - first_row + BAND, 0, ext.shape[0] - 1)]
                        for s in range(slots)
                    ],
                    axis=1,
                )
                blocks = jnp.concatenate(
                    [
                        jnp.concatenate([ref[r, s] for s in range(slots)], axis=1)
                        for ref in (stiff_ref, mass_ref)
                    ],
                    axis=0,
                )
                both = product(picked, blocks, NT)
                applied.append(both[:, :blk] - factor_ref[:, :blk] * both[:, blk:])
            rounded = jnp.concatenate([ext[BAND + 2 * p + q] for q in range(2)], axis=1)
            gap = field[p] - rounded.astype(F32)
            value = load_ref[:, lanes(p)] - jnp.concatenate(applied, axis=1) - dyn_ref[p] * gap
            shift[p] = value
            if carry is None:
                return carry
            return carry + product(stacked(value), hot[lanes(p), :], NN)

        return lax.fori_loop(first * BAND // 2, stop * BAND // 2, body, gathered, unroll=4)

    own = pl.ds(pl.multiple_of(harm * nh, nh), nh)

    def share_copies(k):
        return [
            pltpu.make_async_remote_copy(
                src_ref=shared.at[k, 0, own],
                dst_ref=shared.at[k, 0 if i < harm_size - 1 else 1, own],
                send_sem=share_send.at[k, i],
                recv_sem=share_recv.at[k, i],
                device_id=partner,
                device_id_type=MESH,
            )
            for i, partner in enumerate(partners)
        ]

    def share(k, listed):
        listed_ref[...] = listed
        change = listed if k == 0 else listed - sent_ref[...]
        rounded = change.astype(BF16)
        shared[k, 0, own] = rounded
        for copy in share_copies(k):
            copy.start()
        sent = rounded.astype(F32)
        sent_ref[...] = sent if k == 0 else sent_ref[...] + sent

    def halo_copies(k):
        up = pltpu.make_async_remote_copy(
            src_ref=ext.at[pl.ds(block_rows, BAND)],
            dst_ref=halo.at[k, 0],
            send_sem=halo_send.at[k, 0],
            recv_sem=halo_recv.at[k, 0],
            device_id=(after, harm),
            device_id_type=MESH,
        )
        down = pltpu.make_async_remote_copy(
            src_ref=ext.at[pl.ds(BAND, BAND)],
            dst_ref=halo.at[k, 1],
            send_sem=halo_send.at[k, 1],
            recv_sem=halo_recv.at[k, 1],
            device_id=(before, harm),
            device_id_type=MESH,
        )
        return up, down

    def start_halo(k):
        up, down = halo_copies(k)

        @pl.when(has_next)
        def _():
            up.start()

        @pl.when(has_prev)
        def _():
            down.start()

    share(0, listed)
    start_halo(0)

    for k in range(ITERS):
        up, down = halo_copies(k)
        last = k == ITERS - 1

        def span(first, stop, gathered):
            if k > 0:
                return apply_rows(first, stop, gathered)
            for chunk in range(first, stop):
                for copy in block_copies[chunk]:
                    copy.wait()
                gathered = apply_rows(chunk, chunk + 1, gathered)
            return gathered

        gathered = None if last else jnp.zeros((2 * nh, cmax), F32)
        gathered = span(1, chunks - 1, gathered)

        @pl.when(has_next)
        def _():
            up.wait_send()
            down.wait_recv()
            ext[pl.ds(BAND + block_rows, BAND)] = halo[k, 1]

        @pl.when(has_prev)
        def _():
            down.wait_send()
            up.wait_recv()
            ext[pl.ds(0, BAND)] = halo[k, 0]

        gathered = span(0, 1, gathered)
        gathered = span(chunks - 1, chunks, gathered)

        if k == 0:
            for copy in table_copies:
                copy.wait()
        for copy in share_copies(k):
            copy.wait()
        change = shared[k, 0].astype(F32) - product(shared[k, 1], perm[...], NN)
        relative = change if k == 0 else relative_ref[...] + change
        relative_ref[...] = relative
        rel_parts[...] = stacked(relative * spring_ratio)
        total = jnp.zeros((2 * nh, cmax), F32)
        step_points = 2 * H
        for t in range(0, TIME_POINTS, step_points):
            values = product(time_ref[pl.ds(t, step_points), :], rel_parts[...], NN)
            wave = jnp.tanh(values).astype(BF16)
            total = total + product(back_ref[harm, :, pl.ds(t, step_points)], wave, NN)
        force = folded(total) * own_weight * slot_scale
        projected = stacked(force)
        if not last:
            share(k + 1, listed_ref[...] + (folded(gathered) - force) * slot_inverse[...])

        def finish(p, carry):
            nonlinear = folded(product(projected, hot[lanes(p), :], NT))
            residual = shift[p] - nonlinear
            value = field[p] + residual * inv_ref[p]
            if last:
                disp_out[:, lanes(p)] = value
                res_out[:, lanes(p)] = residual
            else:
                field[p] = value
                put_rounded(p, value)
            return carry

        edge = BAND // 2
        lax.fori_loop(0, edge, finish, 0, unroll=edge)
        lax.fori_loop(pairs - edge, pairs, finish, 0, unroll=edge)
        if not last:
            start_halo(k + 1)
        lax.fori_loop(edge, pairs - edge, finish, 0, unroll=8)


def local(comp_size, harm_size, *arrays):
    load, stiff_blocks, mass_blocks, block_cols = arrays[:4]
    nh, dofs = load.shape
    block_rows, slots, blk, _ = stiff_blocks.shape
    cmax = arrays[4].shape[1]
    to_time, back = host_tables(harm_size)
    vmem = pl.BlockSpec(memory_space=pltpu.VMEM)
    smem = pl.BlockSpec(memory_space=pltpu.SMEM)
    hbm = pl.BlockSpec(memory_space=pltpu.HBM)
    wide = (block_rows // 2, nh, 2 * blk)
    dma = pltpu.SemaphoreType.DMA
    places = [hbm, hbm, hbm, hbm, hbm, hbm, smem, hbm, hbm, smem, hbm, hbm]
    operands = (load, stiff_blocks, mass_blocks, block_cols.T, *arrays[4:], jnp.asarray(to_time), jnp.asarray(back))
    return pl.pallas_call(
        functools.partial(kernel, comp_size, harm_size),
        out_shape=(jax.ShapeDtypeStruct((nh, dofs), F32),) * 2,
        in_specs=places,
        out_specs=(vmem, vmem),
        scratch_shapes=[
            pltpu.SMEM((slots, block_rows), jnp.int32),
            pltpu.VMEM((1, cmax), jnp.int32),
            pltpu.VMEM((1, cmax), jnp.int32),
            pltpu.VMEM((1, cmax), F32),
            pltpu.VMEM((1, cmax), F32),
            pltpu.VMEM((nh, 2 * blk), F32),
            pltpu.VMEM(load.shape, F32),
            pltpu.VMEM(to_time.shape, BF16),
            pltpu.VMEM(back.shape, BF16),
            pltpu.VMEM(stiff_blocks.shape, BF16),
            pltpu.VMEM(mass_blocks.shape, BF16),
            pltpu.VMEM(wide, F32),
            pltpu.VMEM(wide, F32),
            pltpu.VMEM(wide, F32),
            pltpu.VMEM(wide, F32),
            pltpu.VMEM((nh, cmax), F32),
            pltpu.VMEM((dofs, cmax), BF16),
            pltpu.VMEM((cmax, cmax), BF16),
            pltpu.VMEM((block_rows + 2 * BAND, nh, blk), BF16),
            pltpu.VMEM((ITERS, 2, BAND, nh, blk), BF16),
            pltpu.VMEM((nh, cmax), F32),
            pltpu.VMEM((nh, cmax), F32),
            pltpu.VMEM((ITERS, 2, H, cmax), BF16),
            pltpu.VMEM((H, cmax), F32),
            pltpu.VMEM((2 * H, cmax), BF16),
            dma((5,)),
            dma((3,)),
            dma((2,)),
            dma((block_rows // BAND, 2)),
            dma((ITERS, 2)),
            dma((ITERS, 2)),
            dma((ITERS, 2 * harm_size - 1)),
            dma((ITERS, 2 * harm_size - 1)),
        ],
        compiler_params=pltpu.CompilerParams(
            collective_id=0, has_side_effects=True, vmem_limit_bytes=52 * 1024 * 1024
        ),
    )(
        *(
            pltpu.with_memory_space_constraint(value, pltpu.HBM) if where is hbm else value
            for value, where in zip(operands, places)
        )
    )


def solution(mesh):
    placed = (
        P("harm", "comp"),
        P("comp", None, None, None),
        P("comp", None, None, None),
        P("comp", None),
        P("comp", None),
        P("comp", None),
        P("comp"),
        P("comp", None),
        P("comp", None),
        P(),
    )
    return jax.shard_map(
        functools.partial(local, mesh.shape["comp"], mesh.shape["harm"]),
        mesh=mesh,
        in_specs=placed,
        out_specs=(P("harm", "comp"), P("harm", "comp")),
        check_vma=False,
    )
```

```python
import functools
import math

import jax
import jax.numpy as jnp
import numpy as np
from jax import lax
from jax.experimental import pallas as pl
from jax.experimental.pallas import tpu as pltpu
from jax.sharding import PartitionSpec as P

H = 128
TIME_POINTS = 1024
BAND = 8
ITERS = 3
MESH = pl.DeviceIdType.MESH
F32 = jnp.float32
BF16 = jnp.bfloat16
NN = (((1,), (0,)), ((), ()))
NT = (((1,), (1,)), ((), ()))


def host_tables(pair_parts):
    column = np.arange(H)
    orders = np.where(column <= H // 2, column, column - H // 2)
    phase = np.arange(TIME_POINTS)[:, None] * orders[None, :] % TIME_POINTS
    angle = phase * (2.0 * math.pi / TIME_POINTS)
    table = np.where(column[None, :] <= H // 2, np.cos(angle), np.sin(angle))
    table = table.astype(np.float32)
    high = table.astype(BF16)
    low = (table - high.astype(np.float32)).astype(BF16)
    to_time = np.concatenate([high, high], axis=1)
    back = np.stack(
        [high.T.reshape(pair_parts, -1, TIME_POINTS), low.T.reshape(pair_parts, -1, TIME_POINTS)], axis=1
    )
    return to_time, back.reshape(pair_parts, -1, TIME_POINTS)


def halves(value):
    high = value.astype(BF16)
    low = (value - high.astype(F32)).astype(BF16)
    return high, low


def stacked(value):
    return jnp.concatenate(halves(value), axis=0)


def folded(value):
    half = value.shape[0] // 2
    return value[:half] + value[half:]


def product(left, right, dims):
    return lax.dot_general(left, right, dims, preferred_element_type=F32)


def kernel(
    comp_size,
    harm_size,
    load_hbm,
    stiff_hbm,
    mass_hbm,
    cols_hbm,
    rows_hbm,
    partner_hbm,
    count_ref,
    normal_hbm,
    spring_hbm,
    freq_ref,
    time_hbm,
    back_hbm,
    disp_out,
    res_out,
    cols_ref,
    rows_ref,
    partner_ref,
    normal_ref,
    spring_ref,
    factor_ref,
    load_ref,
    time_ref,
    back_ref,
    stiff_ref,
    mass_ref,
    field,
    shift,
    dyn_ref,
    inv_ref,
    slot_inverse,
    hot,
    perm,
    ext,
    halo,
    part_ref,
    mate_part,
    listed_ref,
    sent_ref,
    shared,
    relative_ref,
    rel_parts,
    out_stage,
    small_sem,
    side_sem,
    diag_sem,
    block_sem,
    load_sem,
    halo_send,
    halo_recv,
    part_send,
    part_recv,
    share_send,
    share_recv,
    out_send,
    out_recv,
):
    comp = lax.axis_index("comp")
    harm = lax.axis_index("harm")
    core = lax.rem(harm, 2)
    mate = harm + 1 - 2 * core
    block_rows = stiff_ref.shape[0]
    slots = stiff_ref.shape[1]
    blk = stiff_ref.shape[2]
    both_nh = load_ref.shape[0]
    nh = both_nh // 2
    half = block_rows * blk
    wide = 2 * blk
    pairs = block_rows // 2
    chunks = block_rows // BAND
    span = BAND // 2
    cmax = rows_ref.shape[1]
    row0 = core * block_rows
    first_row = comp * 2 * block_rows + row0
    outer = comp + 2 * core - 1
    has_outer = jnp.logical_and(outer >= 0, outer < comp_size)
    outer = lax.rem(outer + comp_size, comp_size)
    facing = lax.rem(comp + comp_size // 2, comp_size)
    outside = core * (chunks - 1)
    inside = (1 - core) * (chunks - 1)
    middle = list(range(1, chunks - 1))
    order = [inside, *middle, outside]
    first_side = 0
    last_side = BAND + block_rows
    outside_halo = core * last_side
    inside_halo = (1 - core) * last_side

    small_copies = [
        pltpu.make_async_copy(source, held, small_sem.at[i])
        for i, (source, held) in enumerate(
            (
                (rows_hbm, rows_ref),
                (partner_hbm, partner_ref),
                (normal_hbm, normal_ref),
                (spring_hbm, spring_ref),
                (cols_hbm, cols_ref),
            )
        )
    ]
    for copy in small_copies:
        copy.start()
    own_rows = pl.ds(pl.multiple_of(core * nh, nh), nh)
    own_half = pl.ds(pl.multiple_of(core * half, half), half)
    mate_half = pl.ds(pl.multiple_of((1 - core) * half, half), half)
    here = pl.ds(row0, block_rows)
    diag_copies = [
        pltpu.make_async_copy(source.at[here, pl.ds(0, 1)], held.at[:, pl.ds(0, 1)], diag_sem.at[i])
        for i, (source, held) in enumerate(((stiff_hbm, stiff_ref), (mass_hbm, mass_ref)))
    ]
    for copy in diag_copies:
        copy.start()
    load_copy, *table_copies = [
        pltpu.make_async_copy(source, held, side_sem.at[i])
        for i, (source, held) in enumerate(
            (
                (load_hbm.at[:, own_half], load_ref.at[own_rows]),
                (time_hbm, time_ref),
                (back_hbm.at[harm // 2], back_ref),
            )
        )
    ]
    load_copy.start()
    block_copies = []
    for n, c in enumerate(order):
        source_span = (pl.ds(row0 + c * BAND, BAND), pl.ds(1, slots - 1))
        held_span = (pl.ds(c * BAND, BAND), pl.ds(1, slots - 1))
        block_copies.append(
            [
                pltpu.make_async_copy(source.at[source_span], held.at[held_span], block_sem.at[n, i])
                for i, (source, held) in enumerate(((stiff_hbm, stiff_ref), (mass_hbm, mass_ref)))
            ]
        )

    barrier = pltpu.get_barrier_semaphore()
    partners = [(comp, lax.rem(harm + step, harm_size)) for step in range(1, harm_size)]
    partners += [(facing, lax.rem(harm + step, harm_size)) for step in range(harm_size)]
    for partner in partners:
        pl.semaphore_signal(barrier, inc=1, device_id=partner, device_id_type=MESH)

    @pl.when(has_outer)
    def _():
        pl.semaphore_signal(barrier, inc=1, device_id=(outer, mate), device_id_type=MESH)

    for copy in small_copies:
        copy.wait()

    row_list = rows_ref[...]
    sub = lax.broadcasted_iota(jnp.int32, (wide, cmax), 0) + core * half

    def mark(p, carry):
        base = pl.multiple_of(p * wide, wide)
        hot[pl.ds(base, wide), :] = jnp.where(sub == row_list - base, 1.0, 0.0).astype(BF16)
        return carry

    lax.fori_loop(0, pairs, mark, 0, unroll=2)

    pl.semaphore_wait(barrier, len(partners) + has_outer.astype(jnp.int32))
    load_send = pltpu.make_async_remote_copy(
        src_ref=load_hbm.at[:, mate_half],
        dst_ref=load_ref.at[own_rows],
        send_sem=load_sem.at[0],
        recv_sem=load_sem.at[1],
        device_id=(comp, mate),
        device_id_type=MESH,
    )
    load_send.start()

    slot_axis = lax.broadcasted_iota(jnp.int32, (cmax, cmax), 0)
    perm[...] = jnp.where(slot_axis == partner_ref[...], 1.0, 0.0).astype(BF16)

    @pl.when(jnp.logical_not(has_outer))
    def _():
        ext[pl.ds(outside_halo, BAND)] = jnp.zeros((BAND, both_nh, blk), BF16)

    def own_of(value):
        return jnp.where(core == 0, value[:nh], value[nh:])

    def mate_of(value):
        return jnp.where(core == 0, value[nh:], value[:nh])

    def factor_of(start, rows, width):
        index = start + lax.broadcasted_iota(jnp.int32, (rows, width), 0)
        wave = jnp.where(index <= H // 2, index, index - H // 2).astype(F32)
        value = freq_ref[0] * wave * (2.0 / H)
        return value * value

    both_first = (harm - core) * nh
    factor_ref[...] = factor_of(both_first, both_nh, wide)
    slot_index = lax.broadcasted_iota(jnp.int32, (1, cmax), 1)
    slot_scale = jnp.where(slot_index < count_ref[0], normal_ref[...], 0.0)
    both_index = both_first + lax.broadcasted_iota(jnp.int32, (both_nh, cmax), 0)
    weight = jnp.where(both_index == 0, 1.0 / TIME_POINTS, 2.0 / TIME_POINTS)
    spring_ratio = spring_ref[...] / normal_ref[...]

    for copy in diag_copies:
        copy.wait()
    load_copy.wait()
    load_send.wait()
    for copies in block_copies:
        for copy in copies:
            copy.start()
    for copy in table_copies:
        copy.start()
    eye = lax.broadcasted_iota(jnp.int32, (blk, blk), 0) == lax.broadcasted_iota(
        jnp.int32, (blk, blk), 1
    )

    def diagonal(ref, p):
        parts = [
            jnp.sum(jnp.where(eye, ref[2 * p + q, 0].astype(F32), 0.0), axis=0, keepdims=True)
            for q in range(2)
        ]
        return jnp.concatenate(parts, axis=1)

    def put_rounded(p, value):
        rounded = value.astype(BF16)
        for q in range(2):
            ext[BAND + 2 * p + q] = rounded[:, q * blk : (q + 1) * blk]

    def lanes(p):
        return pl.ds(pl.multiple_of(p * wide, wide), wide)

    def start_field(p, gathered):
        stiff_diag = diagonal(stiff_ref, p)
        mass_diag = diagonal(mass_ref, p)
        dynamic = stiff_diag - factor_ref[...] * mass_diag
        inverse = 1.0 / dynamic
        value = load_ref[:, lanes(p)] * inverse
        dyn_ref[p] = dynamic
        inv_ref[p] = inverse
        field[p] = value
        put_rounded(p, value)
        high, low = halves(value)
        diagonals = jnp.concatenate(
            [jnp.broadcast_to(part, (8, wide)) for part in (stiff_diag, mass_diag)], axis=0
        )
        left = jnp.concatenate([high, low, diagonals.astype(BF16)], axis=0)
        return gathered + product(left, hot[lanes(p), :], NN)

    def part_copy(k):
        return pltpu.make_async_remote_copy(
            src_ref=part_ref.at[k, pl.ds(0, nh + 16 if k == 0 else nh)],
            dst_ref=mate_part.at[k, pl.ds(0, nh + 16 if k == 0 else nh)],
            send_sem=part_send.at[k],
            recv_sem=part_recv.at[k],
            device_id=(comp, mate),
            device_id_type=MESH,
        )

    def halo_copies(k):
        out = pltpu.make_async_remote_copy(
            src_ref=ext.at[pl.ds(BAND + outside * BAND, BAND)],
            dst_ref=halo.at[k, 0],
            send_sem=halo_send.at[k, 0],
            recv_sem=halo_recv.at[k, 0],
            device_id=(outer, mate),
            device_id_type=MESH,
        )
        across = pltpu.make_async_remote_copy(
            src_ref=ext.at[pl.ds(BAND + inside * BAND, BAND)],
            dst_ref=halo.at[k, 1],
            send_sem=halo_send.at[k, 1],
            recv_sem=halo_recv.at[k, 1],
            device_id=(comp, mate),
            device_id_type=MESH,
        )
        return out, across

    def start_out(k):
        @pl.when(has_outer)
        def _():
            halo_copies(k)[0].start()

    own = pl.ds(pl.multiple_of(harm * nh, nh), nh)

    def share_copies(k):
        return [
            pltpu.make_async_remote_copy(
                src_ref=shared.at[k, 0, own],
                dst_ref=shared.at[k, 0 if i < harm_size - 1 else 1, own],
                send_sem=share_send.at[k, i],
                recv_sem=share_recv.at[k, i],
                device_id=partner,
                device_id_type=MESH,
            )
            for i, partner in enumerate(partners)
        ]

    def share(k, listed):
        listed_ref[...] = listed
        change = listed if k == 0 else listed - sent_ref[...]
        rounded = change.astype(BF16)
        shared[k, 0, own] = rounded
        for copy in share_copies(k):
            copy.start()
        sent = rounded.astype(F32)
        sent_ref[...] = sent if k == 0 else sent_ref[...] + sent

    def in_order(body, carry, after_outside=None):
        for n, c in enumerate([outside, *middle, inside]):
            carry = lax.fori_loop(0, span, lambda i, now, c=c: body(c * span + i, now), carry, unroll=span)
            if n == 0 and after_outside is not None:
                after_outside()
        return carry

    gathered = in_order(
        start_field, jnp.zeros((2 * both_nh + 16, cmax), F32), lambda: start_out(0)
    )
    listed = folded(gathered[: 2 * both_nh])
    part_ref[0, pl.ds(0, nh)] = mate_of(listed)
    part_ref[0, pl.ds(nh, 16)] = gathered[2 * both_nh :]
    part_copy(0).start()
    halo_copies(0)[1].start()
    listed_ref[...] = own_of(listed)

    def apply_rows(c, gathered):
        def body(i, carry):
            p = c * span + i
            applied = []
            for q in range(2):
                r = 2 * p + q
                picked = jnp.concatenate(
                    [
                        ext[
                            jnp.clip(
                                cols_ref[s, row0 + r] - first_row + BAND, 0, ext.shape[0] - 1
                            )
                        ]
                        for s in range(slots)
                    ],
                    axis=1,
                )
                blocks = jnp.concatenate(
                    [
                        jnp.concatenate([ref[r, s] for s in range(slots)], axis=1)
                        for ref in (stiff_ref, mass_ref)
                    ],
                    axis=0,
                )
                both = product(picked, blocks, NT)
                applied.append(both[:, :blk] - factor_ref[:, :blk] * both[:, blk:])
            rounded = jnp.concatenate([ext[BAND + 2 * p + q] for q in range(2)], axis=1)
            gap = field[p] - rounded.astype(F32)
            value = load_ref[:, lanes(p)] - jnp.concatenate(applied, axis=1) - dyn_ref[p] * gap
            shift[p] = value
            if carry is None:
                return carry
            return carry + product(stacked(value), hot[lanes(p), :], NN)

        return lax.fori_loop(0, span, body, gathered, unroll=span)

    part_copy(0).wait()
    both_parts = part_ref[0, pl.ds(nh, 16)] + mate_part[0, pl.ds(nh, 16)]
    slot_dynamic = both_parts[:1] - factor_of(harm * nh, nh, cmax) * both_parts[8:9]
    slot_inverse[...] = 1.0 / slot_dynamic
    share(0, listed_ref[...] + mate_part[0, pl.ds(0, nh)])

    for k in range(ITERS):
        out, across = halo_copies(k)
        last = k == ITERS - 1

        def take_blocks(n):
            if k == 0:
                for copy in block_copies[n]:
                    copy.wait()

        gathered = None if last else jnp.zeros((2 * both_nh, cmax), F32)
        across.wait()
        ext[pl.ds(inside_halo, BAND)] = halo[k, 1]
        take_blocks(0)
        gathered = apply_rows(inside, gathered)
        for n, c in enumerate(middle):
            take_blocks(1 + n)
            gathered = apply_rows(c, gathered)

        @pl.when(has_outer)
        def _():
            out.wait()
            ext[pl.ds(outside_halo, BAND)] = halo[k, 0]

        take_blocks(chunks - 1)
        gathered = apply_rows(outside, gathered)
        if not last:
            listed = folded(gathered)
            own_part = own_of(listed)
            part_ref[k + 1, pl.ds(0, nh)] = mate_of(listed)
            part_copy(k + 1).start()

        if k == 0:
            for copy in table_copies:
                copy.wait()
        for copy in share_copies(k):
            copy.wait()
        change = shared[k, 0].astype(F32) - product(shared[k, 1], perm[...], NN)
        relative = change if k == 0 else relative_ref[...] + change
        relative_ref[...] = relative
        rel_parts[...] = stacked(relative * spring_ratio)
        total = jnp.zeros((2 * both_nh, cmax), F32)
        step_points = 2 * H
        for t in range(0, TIME_POINTS, step_points):
            values = product(time_ref[pl.ds(t, step_points), :], rel_parts[...], NN)
            wave = jnp.tanh(values).astype(BF16)
            total = total + product(back_ref[:, pl.ds(t, step_points)], wave, NN)
        force = folded(total) * weight * slot_scale
        projected = stacked(force)
        if not last:
            part_copy(k + 1).wait()
            listed = own_part + mate_part[k + 1, pl.ds(0, nh)] - own_of(force)
            share(k + 1, listed_ref[...] + listed * slot_inverse[...])

        def finish(p, carry):
            nonlinear = folded(product(projected, hot[lanes(p), :], NT))
            residual = shift[p] - nonlinear
            value = field[p] + residual * inv_ref[p]
            if last:
                column = pl.ds(pl.multiple_of(core * half + p * wide, wide), wide)
                for n, (target, result) in enumerate(((disp_out, value), (res_out, residual))):
                    target[:, column] = own_of(result)
                    out_stage[n, :, lanes(p)] = mate_of(result)
            else:
                field[p] = value
                put_rounded(p, value)
            return carry

        if last:
            results = []
            for m, c in enumerate(range(chunks)):
                lax.fori_loop(c * span, (c + 1) * span, finish, 0, unroll=span)
                for n, target in enumerate((disp_out, res_out)):
                    width = BAND * blk
                    column = pl.ds(pl.multiple_of(core * half + c * width, width), width)
                    results.append(
                        pltpu.make_async_remote_copy(
                            src_ref=out_stage.at[n, :, pl.ds(c * width, width)],
                            dst_ref=target.at[:, column],
                            send_sem=out_send.at[m, n],
                            recv_sem=out_recv.at[m, n],
                            device_id=(comp, mate),
                            device_id_type=MESH,
                        )
                    )
                    results[-1].start()
            for copy in results:
                copy.wait()
        else:
            in_order(finish, 0, lambda: start_out(k + 1))
            halo_copies(k + 1)[1].start()


def local(comp_size, harm_size, *arrays):
    load, stiff_blocks, mass_blocks, block_cols = arrays[:4]
    nh, dofs = load.shape
    both_nh = 2 * nh
    all_rows, slots, blk, _ = stiff_blocks.shape
    block_rows = all_rows // 2
    held = (block_rows, slots, blk, blk)
    cmax = arrays[4].shape[1]
    to_time, back = host_tables(harm_size // 2)
    vmem = pl.BlockSpec(memory_space=pltpu.VMEM)
    smem = pl.BlockSpec(memory_space=pltpu.SMEM)
    hbm = pl.BlockSpec(memory_space=pltpu.HBM)
    wide = (block_rows // 2, both_nh, 2 * blk)
    dma = pltpu.SemaphoreType.DMA
    places = [hbm, hbm, hbm, hbm, hbm, hbm, smem, hbm, hbm, smem, hbm, hbm]
    operands = (load, stiff_blocks, mass_blocks, block_cols.T, *arrays[4:], jnp.asarray(to_time), jnp.asarray(back))
    return pl.pallas_call(
        functools.partial(kernel, comp_size, harm_size),
        out_shape=(jax.ShapeDtypeStruct((nh, dofs), F32),) * 2,
        in_specs=places,
        out_specs=(vmem, vmem),
        scratch_shapes=[
            pltpu.SMEM((slots, all_rows), jnp.int32),
            pltpu.VMEM((1, cmax), jnp.int32),
            pltpu.VMEM((1, cmax), jnp.int32),
            pltpu.VMEM((1, cmax), F32),
            pltpu.VMEM((1, cmax), F32),
            pltpu.VMEM((both_nh, 2 * blk), F32),
            pltpu.VMEM((both_nh, dofs // 2), F32),
            pltpu.VMEM(to_time.shape, BF16),
            pltpu.VMEM(back.shape[1:], BF16),
            pltpu.VMEM(held, BF16),
            pltpu.VMEM(held, BF16),
            pltpu.VMEM(wide, F32),
            pltpu.VMEM(wide, F32),
            pltpu.VMEM(wide, F32),
            pltpu.VMEM(wide, F32),
            pltpu.VMEM((nh, cmax), F32),
            pltpu.VMEM((dofs // 2, cmax), BF16),
            pltpu.VMEM((cmax, cmax), BF16),
            pltpu.VMEM((block_rows + 2 * BAND, both_nh, blk), BF16),
            pltpu.VMEM((ITERS, 2, BAND, both_nh, blk), BF16),
            pltpu.VMEM((ITERS, nh + 16, cmax), F32),
            pltpu.VMEM((ITERS, nh + 16, cmax), F32),
            pltpu.VMEM((nh, cmax), F32),
            pltpu.VMEM((nh, cmax), F32),
            pltpu.VMEM((ITERS, 2, H, cmax), BF16),
            pltpu.VMEM((H, cmax), F32),
            pltpu.VMEM((2 * H, cmax), BF16),
            pltpu.VMEM((2, nh, dofs // 2), F32),
            dma((5,)),
            dma((3,)),
            dma((2,)),
            dma((block_rows // BAND, 2)),
            dma((2,)),
            dma((ITERS, 2)),
            dma((ITERS, 2)),
            dma((ITERS,)),
            dma((ITERS,)),
            dma((ITERS, 2 * harm_size - 1)),
            dma((ITERS, 2 * harm_size - 1)),
            dma((block_rows // BAND, 2)),
            dma((block_rows // BAND, 2)),
        ],
        compiler_params=pltpu.CompilerParams(
            collective_id=0, has_side_effects=True, vmem_limit_bytes=52 * 1024 * 1024
        ),
    )(
        *(
            pltpu.with_memory_space_constraint(value, pltpu.HBM) if where is hbm else value
            for value, where in zip(operands, places)
        )
    )


def solution(mesh):
    placed = (
        P("harm", "comp"),
        P("comp", None, None, None),
        P("comp", None, None, None),
        P("comp", None),
        P("comp", None),
        P("comp", None),
        P("comp"),
        P("comp", None),
        P("comp", None),
        P(),
    )
    return jax.shard_map(
        functools.partial(local, mesh.shape["comp"], mesh.shape["harm"]),
        mesh=mesh,
        in_specs=placed,
        out_specs=(P("harm", "comp"), P("harm", "comp")),
        check_vma=False,
    )
```

```python
import functools
import math

import jax
import jax.numpy as jnp
import numpy as np
from jax import lax
from jax.experimental import pallas as pl
from jax.experimental.pallas import tpu as pltpu
from jax.sharding import PartitionSpec as P

H = 128
TIME_POINTS = 1024
BAND = 8
ITERS = 3
PIECES = 4
MESH = pl.DeviceIdType.MESH
F32 = jnp.float32
BF16 = jnp.bfloat16
NN = (((1,), (0,)), ((), ()))
NT = (((1,), (1,)), ((), ()))


def host_tables(pair_parts):
    column = np.arange(H)
    orders = np.where(column <= H // 2, column, column - H // 2)
    phase = np.arange(TIME_POINTS)[:, None] * orders[None, :] % TIME_POINTS
    angle = phase * (2.0 * math.pi / TIME_POINTS)
    table = np.where(column[None, :] <= H // 2, np.cos(angle), np.sin(angle))
    table = table.astype(np.float32)
    high = table.astype(BF16)
    low = (table - high.astype(np.float32)).astype(BF16)
    to_time = np.concatenate([high, high], axis=1)
    back = np.stack(
        [high.T.reshape(pair_parts, -1, TIME_POINTS), low.T.reshape(pair_parts, -1, TIME_POINTS)], axis=1
    )
    return to_time, back.reshape(pair_parts, -1, TIME_POINTS)


def halves(value):
    high = value.astype(BF16)
    low = (value - high.astype(F32)).astype(BF16)
    return high, low


def stacked(value):
    return jnp.concatenate(halves(value), axis=0)


def folded(value):
    half = value.shape[0] // 2
    return value[:half] + value[half:]


def product(left, right, dims):
    return lax.dot_general(left, right, dims, preferred_element_type=F32)


def kernel(
    comp_size,
    harm_size,
    load_hbm,
    stiff_hbm,
    mass_hbm,
    cols_hbm,
    rows_hbm,
    partner_hbm,
    normal_hbm,
    spring_hbm,
    time_hbm,
    back_hbm,
    scalars_ref,
    disp_out,
    res_out,
    cols_ref,
    rows_ref,
    partner_ref,
    normal_ref,
    spring_ref,
    factor_ref,
    load_ref,
    time_ref,
    back_ref,
    stiff_ref,
    mass_ref,
    field,
    shift,
    dyn_ref,
    inv_ref,
    slot_inverse,
    hot,
    perm,
    ext,
    halo,
    part_ref,
    mate_part,
    listed_ref,
    sent_ref,
    shared,
    relative_ref,
    rel_parts,
    out_stage,
    small_sem,
    side_sem,
    diag_sem,
    block_sem,
    load_sem,
    halo_send,
    halo_recv,
    part_send,
    part_recv,
    share_send,
    share_recv,
    out_send,
    out_recv,
):
    comp = lax.axis_index("comp")
    harm = lax.axis_index("harm")
    core = lax.rem(harm, 2)
    mate = harm + 1 - 2 * core
    block_rows = stiff_ref.shape[0]
    slots = stiff_ref.shape[1]
    blk = stiff_ref.shape[2]
    both_nh = load_ref.shape[0]
    nh = both_nh // 2
    half = block_rows * blk
    wide = 2 * blk
    pairs = block_rows // 2
    chunks = block_rows // BAND
    span = BAND // 2
    cmax = rows_ref.shape[1]
    row0 = core * block_rows
    first_row = comp * 2 * block_rows + row0
    outer = comp + 2 * core - 1
    has_outer = jnp.logical_and(outer >= 0, outer < comp_size)
    outer = lax.rem(outer + comp_size, comp_size)
    facing = lax.rem(comp + comp_size // 2, comp_size)
    outside = core * (chunks - 1)
    inside = (1 - core) * (chunks - 1)
    middle = list(range(1, chunks - 1))
    order = [inside, *middle, outside]
    first_side = 0
    last_side = BAND + block_rows
    outside_halo = core * last_side
    inside_halo = (1 - core) * last_side

    small_copies = [
        pltpu.make_async_copy(source, held, small_sem.at[i])
        for i, (source, held) in enumerate(
            (
                (rows_hbm, rows_ref),
                (partner_hbm, partner_ref),
                (normal_hbm, normal_ref),
                (spring_hbm, spring_ref),
                (cols_hbm, cols_ref),
            )
        )
    ]
    for copy in small_copies:
        copy.start()
    own_rows = pl.ds(pl.multiple_of(core * nh, nh), nh)
    own_half = pl.ds(pl.multiple_of(core * half, half), half)
    mate_half = pl.ds(pl.multiple_of((1 - core) * half, half), half)
    here = pl.ds(row0, block_rows)
    diag_copies = [
        pltpu.make_async_copy(source.at[here, pl.ds(0, 1)], held.at[:, pl.ds(0, 1)], diag_sem.at[i])
        for i, (source, held) in enumerate(((stiff_hbm, stiff_ref), (mass_hbm, mass_ref)))
    ]
    for copy in diag_copies:
        copy.start()
    load_copy, *table_copies = [
        pltpu.make_async_copy(source, held, side_sem.at[i])
        for i, (source, held) in enumerate(
            (
                (load_hbm.at[:, own_half], load_ref.at[own_rows]),
                (time_hbm, time_ref),
                (back_hbm.at[harm // 2], back_ref),
            )
        )
    ]
    load_copy.start()
    block_copies = []
    for n, c in enumerate(order):
        source_span = (pl.ds(row0 + c * BAND, BAND), pl.ds(1, slots - 1))
        held_span = (pl.ds(c * BAND, BAND), pl.ds(1, slots - 1))
        block_copies.append(
            [
                pltpu.make_async_copy(source.at[source_span], held.at[held_span], block_sem.at[n, i])
                for i, (source, held) in enumerate(((stiff_hbm, stiff_ref), (mass_hbm, mass_ref)))
            ]
        )

    barrier = pltpu.get_barrier_semaphore()
    partners = [(comp, lax.rem(harm + step, harm_size)) for step in range(1, harm_size)]
    partners += [(facing, lax.rem(harm + step, harm_size)) for step in range(harm_size)]
    for partner in partners:
        pl.semaphore_signal(barrier, inc=1, device_id=partner, device_id_type=MESH)

    @pl.when(has_outer)
    def _():
        pl.semaphore_signal(barrier, inc=1, device_id=(outer, mate), device_id_type=MESH)

    pl.semaphore_wait(barrier, len(partners) + has_outer.astype(jnp.int32))
    load_send = pltpu.make_async_remote_copy(
        src_ref=load_hbm.at[:, mate_half],
        dst_ref=load_ref.at[own_rows],
        send_sem=load_sem.at[0],
        recv_sem=load_sem.at[1],
        device_id=(comp, mate),
        device_id_type=MESH,
    )
    load_send.start()

    for copy in small_copies:
        copy.wait()

    row_list = rows_ref[...]
    sub = lax.broadcasted_iota(jnp.int32, (wide, cmax), 0) + core * half

    def mark(p, carry):
        base = pl.multiple_of(p * wide, wide)
        hot[pl.ds(base, wide), :] = jnp.where(sub == row_list - base, 1.0, 0.0).astype(BF16)
        return carry

    lax.fori_loop(0, pairs, mark, 0, unroll=2)

    slot_axis = lax.broadcasted_iota(jnp.int32, (cmax, cmax), 0)
    perm[...] = jnp.where(slot_axis == partner_ref[...], 1.0, 0.0).astype(BF16)

    @pl.when(jnp.logical_not(has_outer))
    def _():
        ext[pl.ds(outside_halo, BAND)] = jnp.zeros((BAND, both_nh, blk), BF16)

    def own_of(value):
        return jnp.where(core == 0, value[:nh], value[nh:])

    def mate_of(value):
        return jnp.where(core == 0, value[nh:], value[:nh])

    def factor_of(start, rows, width):
        index = start + lax.broadcasted_iota(jnp.int32, (rows, width), 0)
        wave = jnp.where(index <= H // 2, index, index - H // 2).astype(F32)
        value = scalars_ref[:1, :width] * wave * (2.0 / H)
        return value * value

    both_first = (harm - core) * nh
    factor_ref[...] = factor_of(both_first, both_nh, wide)
    slot_index = lax.broadcasted_iota(jnp.int32, (1, cmax), 1)
    slot_scale = jnp.where(slot_index.astype(F32) < scalars_ref[1:, :cmax], normal_ref[...], 0.0)
    both_index = both_first + lax.broadcasted_iota(jnp.int32, (both_nh, cmax), 0)
    weight = jnp.where(both_index == 0, 1.0 / TIME_POINTS, 2.0 / TIME_POINTS)
    spring_ratio = spring_ref[...] / normal_ref[...]

    for copy in diag_copies:
        copy.wait()
    eye = lax.broadcasted_iota(jnp.int32, (blk, blk), 0) == lax.broadcasted_iota(
        jnp.int32, (blk, blk), 1
    )

    def diagonal(ref, p):
        parts = [
            jnp.sum(jnp.where(eye, ref[2 * p + q, 0].astype(F32), 0.0), axis=0, keepdims=True)
            for q in range(2)
        ]
        return jnp.concatenate(parts, axis=1)

    def put_rounded(p, value):
        rounded = value.astype(BF16)
        for q in range(2):
            ext[BAND + 2 * p + q] = rounded[:, q * blk : (q + 1) * blk]

    def lanes(p):
        return pl.ds(pl.multiple_of(p * wide, wide), wide)

    def start_diagonal(p, gathered):
        stiff_diag = diagonal(stiff_ref, p)
        mass_diag = diagonal(mass_ref, p)
        dynamic = stiff_diag - factor_ref[...] * mass_diag
        dyn_ref[p] = dynamic
        inv_ref[p] = 1.0 / dynamic
        diagonals = jnp.concatenate(
            [jnp.broadcast_to(part, (8, wide)) for part in (stiff_diag, mass_diag)], axis=0
        )
        return gathered + product(diagonals.astype(BF16), hot[lanes(p), :], NN)

    def start_field(p, gathered):
        value = load_ref[:, lanes(p)] * inv_ref[p]
        field[p] = value
        put_rounded(p, value)
        return gathered + product(stacked(value), hot[lanes(p), :], NN)

    def part_copy(k):
        return pltpu.make_async_remote_copy(
            src_ref=part_ref.at[k, pl.ds(0, nh + 16 if k == 0 else nh)],
            dst_ref=mate_part.at[k, pl.ds(0, nh + 16 if k == 0 else nh)],
            send_sem=part_send.at[k],
            recv_sem=part_recv.at[k],
            device_id=(comp, mate),
            device_id_type=MESH,
        )

    part_rows = BAND // PIECES

    def from_edge(i):
        return jnp.where(core == 0, i, PIECES - 1 - i) * part_rows

    def halo_copies(k):
        pieces = [
            pltpu.make_async_remote_copy(
                src_ref=ext.at[pl.ds(BAND + outside * BAND + from_edge(i), part_rows)],
                dst_ref=halo.at[k, 0, pl.ds(i * part_rows, part_rows)],
                send_sem=halo_send.at[k, 1 + i],
                recv_sem=halo_recv.at[k, 1 + i],
                device_id=(outer, mate),
                device_id_type=MESH,
            )
            for i in range(PIECES)
        ]
        across = pltpu.make_async_remote_copy(
            src_ref=ext.at[pl.ds(BAND + inside * BAND, BAND)],
            dst_ref=halo.at[k, 1],
            send_sem=halo_send.at[k, 0],
            recv_sem=halo_recv.at[k, 0],
            device_id=(comp, mate),
            device_id_type=MESH,
        )
        return pieces, across

    def start_out(k, i):
        @pl.when(has_outer)
        def _():
            halo_copies(k)[0][i].start()

    own = pl.ds(pl.multiple_of(harm * nh, nh), nh)

    def share_copies(k):
        return [
            pltpu.make_async_remote_copy(
                src_ref=shared.at[k, 0, own],
                dst_ref=shared.at[k, 0 if i < harm_size - 1 else 1, own],
                send_sem=share_send.at[k, i],
                recv_sem=share_recv.at[k, i],
                device_id=partner,
                device_id_type=MESH,
            )
            for i, partner in enumerate(partners)
        ]

    def share(k, listed):
        listed_ref[...] = listed
        change = listed if k == 0 else listed - sent_ref[...]
        rounded = change.astype(BF16)
        shared[k, 0, own] = rounded
        for copy in share_copies(k):
            copy.start()
        sent = rounded.astype(F32)
        sent_ref[...] = sent if k == 0 else sent_ref[...] + sent

    def run(body, first, count, carry):
        return lax.fori_loop(0, count, lambda i, now: body(first + i, now), carry, unroll=count)

    def in_order(body, carry, k, then=None):
        for i in range(PIECES):
            first = outside * span + from_edge(i) // 2
            carry = run(body, first, part_rows // 2, carry)
            start_out(k, i)
        if then is not None:
            then()
        for c in [*middle, inside]:
            carry = run(body, c * span, span, carry)
        return carry

    slot_diagonals = lax.fori_loop(
        0, pairs, start_diagonal, jnp.zeros((16, cmax), F32), unroll=span
    )
    part_ref[0, pl.ds(nh, 16)] = slot_diagonals
    load_copy.wait()
    load_send.wait()
    for copies in block_copies:
        for copy in copies:
            copy.start()
    for copy in table_copies:
        copy.start()
    gathered = in_order(start_field, jnp.zeros((2 * both_nh, cmax), F32), 0)
    listed = folded(gathered)
    part_ref[0, pl.ds(0, nh)] = mate_of(listed)
    part_copy(0).start()
    halo_copies(0)[1].start()
    listed_ref[...] = own_of(listed)

    def apply_rows(first, count, gathered):
        def body(p, carry):
            applied = []
            for q in range(2):
                r = 2 * p + q
                picked = jnp.concatenate(
                    [
                        ext[
                            jnp.clip(
                                cols_ref[s, row0 + r] - first_row + BAND, 0, ext.shape[0] - 1
                            )
                        ]
                        for s in range(slots)
                    ],
                    axis=1,
                )
                blocks = jnp.concatenate(
                    [
                        jnp.concatenate([ref[r, s] for s in range(slots)], axis=1)
                        for ref in (stiff_ref, mass_ref)
                    ],
                    axis=0,
                )
                both = product(picked, blocks, NT)
                applied.append(both[:, :blk] - factor_ref[:, :blk] * both[:, blk:])
            rounded = jnp.concatenate([ext[BAND + 2 * p + q] for q in range(2)], axis=1)
            gap = field[p] - rounded.astype(F32)
            value = load_ref[:, lanes(p)] - jnp.concatenate(applied, axis=1) - dyn_ref[p] * gap
            shift[p] = value
            if carry is None:
                return carry
            return carry + product(stacked(value), hot[lanes(p), :], NN)

        return run(body, first, count, gathered)

    part_copy(0).wait()
    both_parts = part_ref[0, pl.ds(nh, 16)] + mate_part[0, pl.ds(nh, 16)]
    slot_dynamic = both_parts[:1] - factor_of(harm * nh, nh, cmax) * both_parts[8:9]
    slot_inverse[...] = 1.0 / slot_dynamic
    share(0, listed_ref[...] + mate_part[0, pl.ds(0, nh)])

    for k in range(ITERS):
        pieces, across = halo_copies(k)
        last = k == ITERS - 1

        def take_blocks(n):
            if k == 0:
                for copy in block_copies[n]:
                    copy.wait()

        gathered = None if last else jnp.zeros((2 * both_nh, cmax), F32)
        across.wait()
        ext[pl.ds(inside_halo, BAND)] = halo[k, 1]
        take_blocks(0)
        gathered = apply_rows(inside * span, span, gathered)
        for n, c in enumerate(middle):
            take_blocks(1 + n)
            gathered = apply_rows(c * span, span, gathered)

        take_blocks(chunks - 1)
        for i, piece in enumerate(pieces):
            to_edge = from_edge(PIECES - 1 - i)

            @pl.when(has_outer)
            def _():
                piece.wait()
                landed = halo[k, 0, pl.ds(i * part_rows, part_rows)]
                ext[pl.ds(outside_halo + to_edge, part_rows)] = landed

            gathered = apply_rows(outside * span + to_edge // 2, part_rows // 2, gathered)

        if not last:
            listed = folded(gathered)
            own_part = own_of(listed)
            part_ref[k + 1, pl.ds(0, nh)] = mate_of(listed)
            part_copy(k + 1).start()

        if k == 0:
            for copy in table_copies:
                copy.wait()
        for copy in share_copies(k):
            copy.wait()
        change = shared[k, 0].astype(F32) - product(shared[k, 1], perm[...], NN)
        relative = change if k == 0 else relative_ref[...] + change
        relative_ref[...] = relative
        rel_parts[...] = stacked(relative * spring_ratio)
        total = jnp.zeros((2 * both_nh, cmax), F32)
        step_points = 2 * H
        for t in range(0, TIME_POINTS, step_points):
            values = product(time_ref[pl.ds(t, step_points), :], rel_parts[...], NN)
            wave = jnp.tanh(values).astype(BF16)
            total = total + product(back_ref[:, pl.ds(t, step_points)], wave, NN)
        force = folded(total) * weight * slot_scale
        projected = stacked(force)
        def finish(p, carry):
            nonlinear = folded(product(projected, hot[lanes(p), :], NT))
            residual = shift[p] - nonlinear
            value = field[p] + residual * inv_ref[p]
            if last:
                column = pl.ds(pl.multiple_of(core * half + p * wide, wide), wide)
                for n, (target, result) in enumerate(((disp_out, value), (res_out, residual))):
                    target[:, column] = own_of(result)
                    out_stage[n, :, lanes(p)] = mate_of(result)
            else:
                field[p] = value
                put_rounded(p, value)
            return carry

        if last:
            results = []
            for m, c in enumerate(range(chunks)):
                lax.fori_loop(c * span, (c + 1) * span, finish, 0, unroll=span)
                for n, target in enumerate((disp_out, res_out)):
                    width = BAND * blk
                    column = pl.ds(pl.multiple_of(core * half + c * width, width), width)
                    results.append(
                        pltpu.make_async_remote_copy(
                            src_ref=out_stage.at[n, :, pl.ds(c * width, width)],
                            dst_ref=target.at[:, column],
                            send_sem=out_send.at[m, n],
                            recv_sem=out_recv.at[m, n],
                            device_id=(comp, mate),
                            device_id_type=MESH,
                        )
                    )
                    results[-1].start()
            for copy in results:
                copy.wait()
        else:

            def send_next():
                part_copy(k + 1).wait()
                listed = own_part + mate_part[k + 1, pl.ds(0, nh)] - own_of(force)
                share(k + 1, listed_ref[...] + listed * slot_inverse[...])

            in_order(finish, 0, k + 1, send_next)
            halo_copies(k + 1)[1].start()


def deliver(disp_ref, res_ref, disp_hbm, res_hbm, sems):
    copies = [
        pltpu.make_async_copy(source, target, sems.at[i])
        for i, (source, target) in enumerate(((disp_ref, disp_hbm), (res_ref, res_hbm)))
    ]
    for copy in copies:
        copy.start()
    for copy in copies:
        copy.wait()


def local(comp_size, harm_size, *arrays):
    load, stiff_blocks, mass_blocks, block_cols = arrays[:4]
    nh, dofs = load.shape
    both_nh = 2 * nh
    all_rows, slots, blk, _ = stiff_blocks.shape
    block_rows = all_rows // 2
    held = (block_rows, slots, blk, blk)
    cmax = arrays[4].shape[1]
    to_time, back = host_tables(harm_size // 2)
    vmem = pl.BlockSpec(memory_space=pltpu.VMEM)
    hbm = pl.BlockSpec(memory_space=pltpu.HBM)
    wide = (block_rows // 2, both_nh, 2 * blk)
    dma = pltpu.SemaphoreType.DMA
    rows, partner, count, normal, spring, freq = arrays[4:]
    width = max(cmax, 2 * blk)
    scalars = jnp.concatenate([jnp.broadcast_to(value.astype(F32), (1, width)) for value in (freq, count)], axis=0)
    operands = (load, stiff_blocks, mass_blocks, block_cols.T, rows, partner, normal, spring)
    operands += (jnp.asarray(to_time), jnp.asarray(back))
    results = pl.pallas_call(
        functools.partial(kernel, comp_size, harm_size),
        out_shape=(jax.ShapeDtypeStruct((nh, dofs), F32),) * 2,
        in_specs=[hbm] * len(operands) + [vmem],
        out_specs=(vmem, vmem),
        scratch_shapes=[
            pltpu.SMEM((slots, all_rows), jnp.int32),
            pltpu.VMEM((1, cmax), jnp.int32),
            pltpu.VMEM((1, cmax), jnp.int32),
            pltpu.VMEM((1, cmax), F32),
            pltpu.VMEM((1, cmax), F32),
            pltpu.VMEM((both_nh, 2 * blk), F32),
            pltpu.VMEM((both_nh, dofs // 2), F32),
            pltpu.VMEM(to_time.shape, BF16),
            pltpu.VMEM(back.shape[1:], BF16),
            pltpu.VMEM(held, BF16),
            pltpu.VMEM(held, BF16),
            pltpu.VMEM(wide, F32),
            pltpu.VMEM(wide, F32),
            pltpu.VMEM(wide, F32),
            pltpu.VMEM(wide, F32),
            pltpu.VMEM((nh, cmax), F32),
            pltpu.VMEM((dofs // 2, cmax), BF16),
            pltpu.VMEM((cmax, cmax), BF16),
            pltpu.VMEM((block_rows + 2 * BAND, both_nh, blk), BF16),
            pltpu.VMEM((ITERS, 2, BAND, both_nh, blk), BF16),
            pltpu.VMEM((ITERS, nh + 16, cmax), F32),
            pltpu.VMEM((ITERS, nh + 16, cmax), F32),
            pltpu.VMEM((nh, cmax), F32),
            pltpu.VMEM((nh, cmax), F32),
            pltpu.VMEM((ITERS, 2, H, cmax), BF16),
            pltpu.VMEM((H, cmax), F32),
            pltpu.VMEM((2 * H, cmax), BF16),
            pltpu.VMEM((2, nh, dofs // 2), F32),
            dma((5,)),
            dma((3,)),
            dma((2,)),
            dma((block_rows // BAND, 2)),
            dma((2,)),
            dma((ITERS, 1 + PIECES)),
            dma((ITERS, 1 + PIECES)),
            dma((ITERS,)),
            dma((ITERS,)),
            dma((ITERS, 2 * harm_size - 1)),
            dma((ITERS, 2 * harm_size - 1)),
            dma((block_rows // BAND, 2)),
            dma((block_rows // BAND, 2)),
        ],
        compiler_params=pltpu.CompilerParams(
            collective_id=0, has_side_effects=True, vmem_limit_bytes=52 * 1024 * 1024
        ),
    )(
        *(pltpu.with_memory_space_constraint(value, pltpu.HBM) for value in operands), scalars
    )
    return pl.pallas_call(
        deliver,
        out_shape=(jax.ShapeDtypeStruct((nh, dofs), F32),) * 2,
        in_specs=[vmem, vmem],
        out_specs=(hbm, hbm),
        scratch_shapes=[dma((2,))],
        compiler_params=pltpu.CompilerParams(vmem_limit_bytes=2 * 1024 * 1024),
    )(*(pltpu.with_memory_space_constraint(value, pltpu.VMEM) for value in results))


def solution(mesh):
    placed = (
        P("harm", "comp"),
        P("comp", None, None, None),
        P("comp", None, None, None),
        P("comp", None),
        P("comp", None),
        P("comp", None),
        P("comp"),
        P("comp", None),
        P("comp", None),
        P(),
    )
    return jax.shard_map(
        functools.partial(local, mesh.shape["comp"], mesh.shape["harm"]),
        mesh=mesh,
        in_specs=placed,
        out_specs=(P("harm", "comp"), P("harm", "comp")),
        check_vma=False,
    )
```

```python
import functools
import math

import jax
import jax.numpy as jnp
import numpy as np
from jax import lax
from jax.experimental import pallas as pl
from jax.experimental.pallas import tpu as pltpu
from jax.sharding import PartitionSpec as P

H = 128
TIME_POINTS = 1024
BAND = 8
ITERS = 3
PIECES = 4
MESH = pl.DeviceIdType.MESH
F32 = jnp.float32
BF16 = jnp.bfloat16
NN = (((1,), (0,)), ((), ()))
NT = (((1,), (1,)), ((), ()))


def host_tables(pair_parts):
    column = np.arange(H)
    orders = np.where(column <= H // 2, column, column - H // 2)
    phase = np.arange(TIME_POINTS)[:, None] * orders[None, :] % TIME_POINTS
    angle = phase * (2.0 * math.pi / TIME_POINTS)
    table = np.where(column[None, :] <= H // 2, np.cos(angle), np.sin(angle))
    table = table.astype(np.float32)
    high = table.astype(BF16)
    low = (table - high.astype(np.float32)).astype(BF16)
    to_time = np.concatenate([high, high], axis=1)
    back = np.stack(
        [high.T.reshape(pair_parts, -1, TIME_POINTS), low.T.reshape(pair_parts, -1, TIME_POINTS)], axis=1
    )
    return to_time, back.reshape(pair_parts, -1, TIME_POINTS)


def halves(value):
    high = value.astype(BF16)
    low = (value - high.astype(F32)).astype(BF16)
    return high, low


def stacked(value):
    return jnp.concatenate(halves(value), axis=0)


def folded(value):
    half = value.shape[0] // 2
    return value[:half] + value[half:]


def product(left, right, dims):
    return lax.dot_general(left, right, dims, preferred_element_type=F32)


def kernel(
    comp_size,
    harm_size,
    load_hbm,
    stiff_hbm,
    mass_hbm,
    cols_hbm,
    rows_hbm,
    partner_hbm,
    normal_hbm,
    spring_hbm,
    time_hbm,
    back_hbm,
    scalars_ref,
    disp_out,
    res_out,
    cols_ref,
    rows_ref,
    partner_ref,
    normal_ref,
    spring_ref,
    factor_ref,
    load_ref,
    time_ref,
    back_ref,
    stiff_ref,
    mass_ref,
    field,
    shift,
    dyn_ref,
    inv_ref,
    slot_inverse,
    hot,
    perm,
    ext,
    halo,
    part_ref,
    mate_part,
    listed_ref,
    sent_ref,
    shared,
    relative_ref,
    rel_parts,
    out_stage,
    small_sem,
    side_sem,
    diag_sem,
    block_sem,
    load_sem,
    halo_send,
    halo_recv,
    part_send,
    part_recv,
    share_send,
    share_recv,
    forward_send,
    forward_recv,
    out_send,
    out_recv,
):
    comp = lax.axis_index("comp")
    harm = lax.axis_index("harm")
    core = lax.rem(harm, 2)
    mate = harm + 1 - 2 * core
    block_rows = stiff_ref.shape[0]
    slots = stiff_ref.shape[1]
    blk = stiff_ref.shape[2]
    both_nh = load_ref.shape[0]
    nh = both_nh // 2
    half = block_rows * blk
    wide = 2 * blk
    pairs = block_rows // 2
    chunks = block_rows // BAND
    span = BAND // 2
    cmax = rows_ref.shape[1]
    row0 = core * block_rows
    first_row = comp * 2 * block_rows + row0
    outer = comp + 2 * core - 1
    has_outer = jnp.logical_and(outer >= 0, outer < comp_size)
    outer = lax.rem(outer + comp_size, comp_size)
    facing = lax.rem(comp + comp_size // 2, comp_size)
    outside = core * (chunks - 1)
    inside = (1 - core) * (chunks - 1)
    middle = list(range(1, chunks - 1))
    order = [inside, *middle, outside]
    first_side = 0
    last_side = BAND + block_rows
    outside_halo = core * last_side
    inside_halo = (1 - core) * last_side

    small_copies = [
        pltpu.make_async_copy(source, held, small_sem.at[i])
        for i, (source, held) in enumerate(
            (
                (rows_hbm, rows_ref),
                (partner_hbm, partner_ref),
                (normal_hbm, normal_ref),
                (spring_hbm, spring_ref),
                (cols_hbm, cols_ref),
            )
        )
    ]
    for copy in small_copies:
        copy.start()
    own_rows = pl.ds(pl.multiple_of(core * nh, nh), nh)
    own_half = pl.ds(pl.multiple_of(core * half, half), half)
    mate_half = pl.ds(pl.multiple_of((1 - core) * half, half), half)
    here = pl.ds(row0, block_rows)
    diag_copies = [
        pltpu.make_async_copy(source.at[here, pl.ds(0, 1)], held.at[:, pl.ds(0, 1)], diag_sem.at[i])
        for i, (source, held) in enumerate(((stiff_hbm, stiff_ref), (mass_hbm, mass_ref)))
    ]
    for copy in diag_copies:
        copy.start()
    load_copy, *table_copies = [
        pltpu.make_async_copy(source, held, side_sem.at[i])
        for i, (source, held) in enumerate(
            (
                (load_hbm.at[:, own_half], load_ref.at[own_rows]),
                (time_hbm, time_ref),
                (back_hbm.at[harm // 2], back_ref),
            )
        )
    ]
    load_copy.start()
    block_copies = []
    for n, c in enumerate(order):
        source_span = (pl.ds(row0 + c * BAND, BAND), pl.ds(1, slots - 1))
        held_span = (pl.ds(c * BAND, BAND), pl.ds(1, slots - 1))
        block_copies.append(
            [
                pltpu.make_async_copy(source.at[source_span], held.at[held_span], block_sem.at[n, i])
                for i, (source, held) in enumerate(((stiff_hbm, stiff_ref), (mass_hbm, mass_ref)))
            ]
        )

    barrier = pltpu.get_barrier_semaphore()
    partners = [(comp, lax.rem(harm + step, harm_size)) for step in range(1, harm_size)]
    partners += [(facing, lax.rem(harm + step, harm_size)) for step in range(harm_size)]
    for partner in partners:
        pl.semaphore_signal(barrier, inc=1, device_id=partner, device_id_type=MESH)

    @pl.when(has_outer)
    def _():
        pl.semaphore_signal(barrier, inc=1, device_id=(outer, mate), device_id_type=MESH)

    pl.semaphore_wait(barrier, len(partners) + has_outer.astype(jnp.int32))
    load_send = pltpu.make_async_remote_copy(
        src_ref=load_hbm.at[:, mate_half],
        dst_ref=load_ref.at[own_rows],
        send_sem=load_sem.at[0],
        recv_sem=load_sem.at[1],
        device_id=(comp, mate),
        device_id_type=MESH,
    )
    load_send.start()

    for copy in small_copies:
        copy.wait()

    row_list = rows_ref[...]
    sub = lax.broadcasted_iota(jnp.int32, (wide, cmax), 0) + core * half

    def mark(p, carry):
        base = pl.multiple_of(p * wide, wide)
        hot[pl.ds(base, wide), :] = jnp.where(sub == row_list - base, 1.0, 0.0).astype(BF16)
        return carry

    lax.fori_loop(0, pairs, mark, 0, unroll=2)

    slot_axis = lax.broadcasted_iota(jnp.int32, (cmax, cmax), 0)
    perm[...] = jnp.where(slot_axis == partner_ref[...], 1.0, 0.0).astype(BF16)

    @pl.when(jnp.logical_not(has_outer))
    def _():
        ext[pl.ds(outside_halo, BAND)] = jnp.zeros((BAND, both_nh, blk), BF16)

    def own_of(value):
        return jnp.where(core == 0, value[:nh], value[nh:])

    def mate_of(value):
        return jnp.where(core == 0, value[nh:], value[:nh])

    def factor_of(start, rows, width):
        index = start + lax.broadcasted_iota(jnp.int32, (rows, width), 0)
        wave = jnp.where(index <= H // 2, index, index - H // 2).astype(F32)
        value = scalars_ref[:1, :width] * wave * (2.0 / H)
        return value * value

    both_first = (harm - core) * nh
    factor_ref[...] = factor_of(both_first, both_nh, wide)
    slot_index = lax.broadcasted_iota(jnp.int32, (1, cmax), 1)
    slot_scale = jnp.where(slot_index.astype(F32) < scalars_ref[1:, :cmax], normal_ref[...], 0.0)
    both_index = both_first + lax.broadcasted_iota(jnp.int32, (both_nh, cmax), 0)
    weight = jnp.where(both_index == 0, 1.0 / TIME_POINTS, 2.0 / TIME_POINTS)
    spring_ratio = spring_ref[...] / normal_ref[...]

    for copy in diag_copies:
        copy.wait()
    eye = lax.broadcasted_iota(jnp.int32, (blk, blk), 0) == lax.broadcasted_iota(
        jnp.int32, (blk, blk), 1
    )

    def diagonal(ref, p):
        parts = [
            jnp.sum(jnp.where(eye, ref[2 * p + q, 0].astype(F32), 0.0), axis=0, keepdims=True)
            for q in range(2)
        ]
        return jnp.concatenate(parts, axis=1)

    def put_rounded(p, value):
        rounded = value.astype(BF16)
        for q in range(2):
            ext[BAND + 2 * p + q] = rounded[:, q * blk : (q + 1) * blk]

    def lanes(p):
        return pl.ds(pl.multiple_of(p * wide, wide), wide)

    def start_diagonal(p, gathered):
        stiff_diag = diagonal(stiff_ref, p)
        mass_diag = diagonal(mass_ref, p)
        dynamic = stiff_diag - factor_ref[...] * mass_diag
        dyn_ref[p] = dynamic
        inv_ref[p] = 1.0 / dynamic
        diagonals = jnp.concatenate(
            [jnp.broadcast_to(part, (8, wide)) for part in (stiff_diag, mass_diag)], axis=0
        )
        return gathered + product(diagonals.astype(BF16), hot[lanes(p), :], NN)

    def start_field(p, gathered):
        value = load_ref[:, lanes(p)] * inv_ref[p]
        field[p] = value
        put_rounded(p, value)
        return gathered + product(stacked(value), hot[lanes(p), :], NN)

    def part_copy(k):
        return pltpu.make_async_remote_copy(
            src_ref=part_ref.at[k, pl.ds(0, nh + 16 if k == 0 else nh)],
            dst_ref=mate_part.at[k, pl.ds(0, nh + 16 if k == 0 else nh)],
            send_sem=part_send.at[k],
            recv_sem=part_recv.at[k],
            device_id=(comp, mate),
            device_id_type=MESH,
        )

    part_rows = BAND // PIECES

    def from_edge(i):
        return jnp.where(core == 0, i, PIECES - 1 - i) * part_rows

    def halo_copies(k):
        pieces = [
            pltpu.make_async_remote_copy(
                src_ref=ext.at[pl.ds(BAND + outside * BAND + from_edge(i), part_rows)],
                dst_ref=halo.at[k, 0, pl.ds(i * part_rows, part_rows)],
                send_sem=halo_send.at[k, 1 + i],
                recv_sem=halo_recv.at[k, 1 + i],
                device_id=(outer, mate),
                device_id_type=MESH,
            )
            for i in range(PIECES)
        ]
        across = pltpu.make_async_remote_copy(
            src_ref=ext.at[pl.ds(BAND + inside * BAND, BAND)],
            dst_ref=halo.at[k, 1],
            send_sem=halo_send.at[k, 0],
            recv_sem=halo_recv.at[k, 0],
            device_id=(comp, mate),
            device_id_type=MESH,
        )
        return pieces, across

    def start_out(k, i):
        @pl.when(has_outer)
        def _():
            halo_copies(k)[0][i].start()

    own = pl.ds(pl.multiple_of(harm * nh, nh), nh)

    same_core = [lax.rem(harm + 2 * step, harm_size) for step in range(harm_size // 2)]
    holders = [(0, comp, index) for index in same_core] + [(1, facing, index) for index in same_core]

    def share_copies(k):
        return [
            pltpu.make_async_remote_copy(
                src_ref=shared.at[k, 0, own],
                dst_ref=shared.at[k, group, own],
                send_sem=share_send.at[k, i],
                recv_sem=share_recv.at[k, i],
                device_id=(place, index),
                device_id_type=MESH,
            )
            for i, (group, place, index) in enumerate(holders[1:])
        ]

    def forward_copies(k):
        copies = []
        for i, (group, _, index) in enumerate(holders):
            rows = pl.ds(pl.multiple_of(index * nh, nh), nh)
            copies.append(
                pltpu.make_async_remote_copy(
                    src_ref=shared.at[k, group, rows],
                    dst_ref=shared.at[k, group, rows],
                    send_sem=forward_send.at[k, i],
                    recv_sem=forward_recv.at[k, i],
                    device_id=(comp, mate),
                    device_id_type=MESH,
                )
            )
        return copies

    def share(k, listed):
        listed_ref[...] = listed
        change = listed if k == 0 else listed - sent_ref[...]
        rounded = change.astype(BF16)
        shared[k, 0, own] = rounded
        for copy in share_copies(k):
            copy.start()
        sent = rounded.astype(F32)
        sent_ref[...] = sent if k == 0 else sent_ref[...] + sent

    def run(body, first, count, carry):
        return lax.fori_loop(0, count, lambda i, now: body(first + i, now), carry, unroll=count)

    def in_order(body, carry, k, then=None):
        for i in range(PIECES):
            first = outside * span + from_edge(i) // 2
            carry = run(body, first, part_rows // 2, carry)
            start_out(k, i)
        if then is not None:
            then()
        for c in [*middle, inside]:
            carry = run(body, c * span, span, carry)
        return carry

    slot_diagonals = lax.fori_loop(
        0, pairs, start_diagonal, jnp.zeros((16, cmax), F32), unroll=span
    )
    part_ref[0, pl.ds(nh, 16)] = slot_diagonals
    load_copy.wait()
    load_send.wait()
    for copies in block_copies:
        for copy in copies:
            copy.start()
    for copy in table_copies:
        copy.start()
    gathered = in_order(start_field, jnp.zeros((2 * both_nh, cmax), F32), 0)
    listed = folded(gathered)
    part_ref[0, pl.ds(0, nh)] = mate_of(listed)
    part_copy(0).start()
    halo_copies(0)[1].start()
    listed_ref[...] = own_of(listed)

    def apply_rows(first, count, gathered):
        def body(p, carry):
            applied = []
            for q in range(2):
                r = 2 * p + q
                picked = jnp.concatenate(
                    [
                        ext[
                            jnp.clip(
                                cols_ref[s, row0 + r] - first_row + BAND, 0, ext.shape[0] - 1
                            )
                        ]
                        for s in range(slots)
                    ],
                    axis=1,
                )
                blocks = jnp.concatenate(
                    [
                        jnp.concatenate([ref[r, s] for s in range(slots)], axis=1)
                        for ref in (stiff_ref, mass_ref)
                    ],
                    axis=0,
                )
                both = product(picked, blocks, NT)
                applied.append(both[:, :blk] - factor_ref[:, :blk] * both[:, blk:])
            rounded = jnp.concatenate([ext[BAND + 2 * p + q] for q in range(2)], axis=1)
            gap = field[p] - rounded.astype(F32)
            value = load_ref[:, lanes(p)] - jnp.concatenate(applied, axis=1) - dyn_ref[p] * gap
            shift[p] = value
            if carry is None:
                return carry
            return carry + product(stacked(value), hot[lanes(p), :], NN)

        return run(body, first, count, gathered)

    part_copy(0).wait()
    both_parts = part_ref[0, pl.ds(nh, 16)] + mate_part[0, pl.ds(nh, 16)]
    slot_dynamic = both_parts[:1] - factor_of(harm * nh, nh, cmax) * both_parts[8:9]
    slot_inverse[...] = 1.0 / slot_dynamic
    share(0, listed_ref[...] + mate_part[0, pl.ds(0, nh)])

    for k in range(ITERS):
        pieces, across = halo_copies(k)
        last = k == ITERS - 1

        def take_blocks(n):
            if k == 0:
                for copy in block_copies[n]:
                    copy.wait()

        gathered = None if last else jnp.zeros((2 * both_nh, cmax), F32)
        across.wait()
        ext[pl.ds(inside_halo, BAND)] = halo[k, 1]
        take_blocks(0)
        gathered = apply_rows(inside * span, span, gathered)
        for n, c in enumerate(middle):
            take_blocks(1 + n)
            gathered = apply_rows(c * span, span, gathered)

        take_blocks(chunks - 1)
        for i, piece in enumerate(pieces):
            to_edge = from_edge(PIECES - 1 - i)

            @pl.when(has_outer)
            def _():
                piece.wait()
                landed = halo[k, 0, pl.ds(i * part_rows, part_rows)]
                ext[pl.ds(outside_halo + to_edge, part_rows)] = landed

            gathered = apply_rows(outside * span + to_edge // 2, part_rows // 2, gathered)
            if i == 1:
                for copy in share_copies(k):
                    copy.wait()
                for copy in forward_copies(k):
                    copy.start()

        if not last:
            listed = folded(gathered)
            own_part = own_of(listed)
            part_ref[k + 1, pl.ds(0, nh)] = mate_of(listed)
            part_copy(k + 1).start()

        if k == 0:
            for copy in table_copies:
                copy.wait()
        for copy in forward_copies(k):
            copy.wait()
        change = shared[k, 0].astype(F32) - product(shared[k, 1], perm[...], NN)
        relative = change if k == 0 else relative_ref[...] + change
        relative_ref[...] = relative
        rel_parts[...] = stacked(relative * spring_ratio)
        total = jnp.zeros((2 * both_nh, cmax), F32)
        step_points = 2 * H
        for t in range(0, TIME_POINTS, step_points):
            values = product(time_ref[pl.ds(t, step_points), :], rel_parts[...], NN)
            wave = jnp.tanh(values).astype(BF16)
            total = total + product(back_ref[:, pl.ds(t, step_points)], wave, NN)
        force = folded(total) * weight * slot_scale
        projected = stacked(force)
        def finish(p, carry):
            nonlinear = folded(product(projected, hot[lanes(p), :], NT))
            residual = shift[p] - nonlinear
            value = field[p] + residual * inv_ref[p]
            if last:
                column = pl.ds(pl.multiple_of(core * half + p * wide, wide), wide)
                for n, (target, result) in enumerate(((disp_out, value), (res_out, residual))):
                    target[:, column] = own_of(result)
                    out_stage[n, :, lanes(p)] = mate_of(result)
            else:
                field[p] = value
                put_rounded(p, value)
            return carry

        if last:
            results = []
            for m, c in enumerate(range(chunks)):
                lax.fori_loop(c * span, (c + 1) * span, finish, 0, unroll=span)
                for n, target in enumerate((disp_out, res_out)):
                    width = BAND * blk
                    column = pl.ds(pl.multiple_of(core * half + c * width, width), width)
                    results.append(
                        pltpu.make_async_remote_copy(
                            src_ref=out_stage.at[n, :, pl.ds(c * width, width)],
                            dst_ref=target.at[:, column],
                            send_sem=out_send.at[m, n],
                            recv_sem=out_recv.at[m, n],
                            device_id=(comp, mate),
                            device_id_type=MESH,
                        )
                    )
                    results[-1].start()
            for copy in results:
                copy.wait()
        else:

            def send_next():
                part_copy(k + 1).wait()
                listed = own_part + mate_part[k + 1, pl.ds(0, nh)] - own_of(force)
                share(k + 1, listed_ref[...] + listed * slot_inverse[...])

            send_next()
            in_order(finish, 0, k + 1)
            halo_copies(k + 1)[1].start()


def deliver(disp_ref, res_ref, disp_hbm, res_hbm, sems):
    copies = [
        pltpu.make_async_copy(source, target, sems.at[i])
        for i, (source, target) in enumerate(((disp_ref, disp_hbm), (res_ref, res_hbm)))
    ]
    for copy in copies:
        copy.start()
    for copy in copies:
        copy.wait()


def local(comp_size, harm_size, *arrays):
    load, stiff_blocks, mass_blocks, block_cols = arrays[:4]
    nh, dofs = load.shape
    both_nh = 2 * nh
    all_rows, slots, blk, _ = stiff_blocks.shape
    block_rows = all_rows // 2
    held = (block_rows, slots, blk, blk)
    cmax = arrays[4].shape[1]
    to_time, back = host_tables(harm_size // 2)
    vmem = pl.BlockSpec(memory_space=pltpu.VMEM)
    hbm = pl.BlockSpec(memory_space=pltpu.HBM)
    wide = (block_rows // 2, both_nh, 2 * blk)
    dma = pltpu.SemaphoreType.DMA
    rows, partner, count, normal, spring, freq = arrays[4:]
    width = max(cmax, 2 * blk)
    scalars = jnp.concatenate([jnp.broadcast_to(value.astype(F32), (1, width)) for value in (freq, count)], axis=0)
    operands = (load, stiff_blocks, mass_blocks, block_cols.T, rows, partner, normal, spring)
    operands += (jnp.asarray(to_time), jnp.asarray(back))
    results = pl.pallas_call(
        functools.partial(kernel, comp_size, harm_size),
        out_shape=(jax.ShapeDtypeStruct((nh, dofs), F32),) * 2,
        in_specs=[hbm] * len(operands) + [vmem],
        out_specs=(vmem, vmem),
        scratch_shapes=[
            pltpu.SMEM((slots, all_rows), jnp.int32),
            pltpu.VMEM((1, cmax), jnp.int32),
            pltpu.VMEM((1, cmax), jnp.int32),
            pltpu.VMEM((1, cmax), F32),
            pltpu.VMEM((1, cmax), F32),
            pltpu.VMEM((both_nh, 2 * blk), F32),
            pltpu.VMEM((both_nh, dofs // 2), F32),
            pltpu.VMEM(to_time.shape, BF16),
            pltpu.VMEM(back.shape[1:], BF16),
            pltpu.VMEM(held, BF16),
            pltpu.VMEM(held, BF16),
            pltpu.VMEM(wide, F32),
            pltpu.VMEM(wide, F32),
            pltpu.VMEM(wide, F32),
            pltpu.VMEM(wide, F32),
            pltpu.VMEM((nh, cmax), F32),
            pltpu.VMEM((dofs // 2, cmax), BF16),
            pltpu.VMEM((cmax, cmax), BF16),
            pltpu.VMEM((block_rows + 2 * BAND, both_nh, blk), BF16),
            pltpu.VMEM((ITERS, 2, BAND, both_nh, blk), BF16),
            pltpu.VMEM((ITERS, nh + 16, cmax), F32),
            pltpu.VMEM((ITERS, nh + 16, cmax), F32),
            pltpu.VMEM((nh, cmax), F32),
            pltpu.VMEM((nh, cmax), F32),
            pltpu.VMEM((ITERS, 2, H, cmax), BF16),
            pltpu.VMEM((H, cmax), F32),
            pltpu.VMEM((2 * H, cmax), BF16),
            pltpu.VMEM((2, nh, dofs // 2), F32),
            dma((5,)),
            dma((3,)),
            dma((2,)),
            dma((block_rows // BAND, 2)),
            dma((2,)),
            dma((ITERS, 1 + PIECES)),
            dma((ITERS, 1 + PIECES)),
            dma((ITERS,)),
            dma((ITERS,)),
            dma((ITERS, harm_size - 1)),
            dma((ITERS, harm_size - 1)),
            dma((ITERS, harm_size)),
            dma((ITERS, harm_size)),
            dma((block_rows // BAND, 2)),
            dma((block_rows // BAND, 2)),
        ],
        compiler_params=pltpu.CompilerParams(
            collective_id=0, has_side_effects=True, vmem_limit_bytes=52 * 1024 * 1024
        ),
    )(
        *(pltpu.with_memory_space_constraint(value, pltpu.HBM) for value in operands), scalars
    )
    return pl.pallas_call(
        deliver,
        out_shape=(jax.ShapeDtypeStruct((nh, dofs), F32),) * 2,
        in_specs=[vmem, vmem],
        out_specs=(hbm, hbm),
        scratch_shapes=[dma((2,))],
        compiler_params=pltpu.CompilerParams(vmem_limit_bytes=2 * 1024 * 1024),
    )(*(pltpu.with_memory_space_constraint(value, pltpu.VMEM) for value in results))


def solution(mesh):
    placed = (
        P("harm", "comp"),
        P("comp", None, None, None),
        P("comp", None, None, None),
        P("comp", None),
        P("comp", None),
        P("comp", None),
        P("comp"),
        P("comp", None),
        P("comp", None),
        P(),
    )
    return jax.shard_map(
        functools.partial(local, mesh.shape["comp"], mesh.shape["harm"]),
        mesh=mesh,
        in_specs=placed,
        out_specs=(P("harm", "comp"), P("harm", "comp")),
        check_vma=False,
    )
```
